32 devices in a mesh: group: 8 (over z, x), sub: 4 (over y, core).
Axes of the slice: x: 2, y: 2, z: 4, core: 2. Of those that a mesh axis runs over, the one named last changes fastest.
Arguments:
- embeddings: bfloat16 [65536, 768], P(('group', 'sub'))
- labels: int32 [512], P(('group', 'sub')), may hold values from 0 to 1, as said below
- group_bit: int32 [1], replicated, may hold values from 0 to 2
- init_index: int32 [8, 128], P('group'), may hold values from 0 to 8191
Outputs:
- centroids: float32 [8, 128, 768], P('group')
- counts: float32 [8, 128], P('group')
The draws below stay inside these ranges and needn't reach their ends.
Inputs may be any that keep to these rules, and one draw needn't show every extreme that they name: `labels`: each label is a child, 0 or 1. `init_index`: row numbers within group g, counted along the sub axis in order.
All inputs are finite; a program needn't handle non-finite values.
Results may differ from the reference program's by a relative error of at most 0.0031.
Values may be sent and summed in bfloat16 or wider, within the bound.
No kernel may reach another device: no remote copies, remote signals or barrier semaphores. Data moves between devices by JAX's collectives and lax.ppermute only.
A program may use at most 64 MiB of HBM per device.

```python
import jax
import jax.numpy as jnp
from jax import lax

EMBED_WIDTH = 768
K = 128
BLOCK = 128
ITERS = 2
ROW_DEV = 2048
ROWS = 65536
N_GROUP = 8
N_SUB = 4
DEVICES = 32


def draw_embeddings(key, part):
    key_base = jax.random.fold_in(key, 11)
    values = jax.random.normal(key_base, (ROWS, EMBED_WIDTH), jnp.float32)
    return values.astype(jnp.bfloat16)


def draw_labels(key, part):
    key_level = jax.random.fold_in(key, 21)
    key_draws = jax.random.fold_in(key, 22)
    thresholds = jax.random.randint(key_level, (DEVICES, 1), 1, 10)
    draws = jax.random.randint(key_draws, (DEVICES, ROW_DEV // BLOCK), 0, 10)
    return (draws < thresholds).astype(jnp.int32).reshape(-1)


def plant(drawn, own_key, smallest, top_value):
    longest = drawn.shape.index(max(drawn.shape))
    spots = []
    for shift in (0, 1):
        where = [jax.random.randint(jax.random.fold_in(own_key, axis), (), 0, length) for axis, length in enumerate(drawn.shape)]
        where[longest] = (where[longest] + shift) % drawn.shape[longest]
        spots.append(tuple(where))
    return drawn.at[spots[0]].set(smallest).at[spots[1]].set(top_value)


def setup_inputs(seed: int = 0) -> dict:
    key_list = jax.random.split(jax.random.key(seed), 5)
    return {
        "embeddings": draw_embeddings(jax.random.fold_in(key_list[4], 71), 0),
        "labels": draw_labels(jax.random.fold_in(key_list[4], 71), 0),
        "group_bit": jax.random.randint(key_list[2], (1,), 0, 3).astype(jnp.int32),
        "init_index": plant(jax.random.randint(key_list[3], (N_GROUP, K), 0, ROW_DEV * N_SUB), jax.random.fold_in(key_list[3], 1), 0, (ROW_DEV * N_SUB) - 1).astype(jnp.int32),
    }


prior_weight = 1.0


def responsibility_terms(candidate_rows, retained_rows, centroids, softness_scale):
    cent_half = centroids.astype(jnp.bfloat16)
    centroid_norm_values = jnp.sum(jnp.square(cent_half.astype(jnp.float32)), axis=1)
    distance_scores = jnp.dot(candidate_rows, cent_half.T, preferred_element_type=jnp.float32)
    assignment_logits = (2.0 * distance_scores - centroid_norm_values[None, :]) / softness_scale
    weights = jax.nn.softmax(assignment_logits, axis=1).astype(jnp.bfloat16) * retained_rows[:, None]
    weighted_totals = jnp.dot(weights.T, candidate_rows, preferred_element_type=jnp.float32)
    counts = jnp.sum(weights.astype(jnp.float32), axis=0)
    return weighted_totals, counts


def reference(embeddings, labels, group_bit, init_index):
    group_rows = ROW_DEV * N_SUB
    grouped = embeddings.reshape(N_GROUP, group_rows, EMBED_WIDTH)
    group_marks = labels.reshape(N_GROUP, group_rows // BLOCK)
    chosen = group_bit[0].astype(jnp.int32)
    softness_scale = EMBED_WIDTH / 8.0

    def one_group(group_id):
        partner = jnp.bitwise_xor(group_id, jnp.left_shift(jnp.int32(1), chosen))
        own_side = jnp.bitwise_and(jnp.right_shift(group_id, chosen), 1)
        own_rows = lax.dynamic_index_in_dim(grouped, group_id, 0, keepdims=False)
        other_rows = lax.dynamic_index_in_dim(grouped, partner, 0, keepdims=False)
        candidate_rows = jnp.concatenate([own_rows, other_rows], axis=0)
        own_marks = lax.dynamic_index_in_dim(group_marks, group_id, 0, keepdims=False)
        other_marks = lax.dynamic_index_in_dim(group_marks, partner, 0, keepdims=False)
        marks = jnp.concatenate([own_marks, other_marks], axis=0)
        retained_rows = jnp.repeat((marks == own_side).astype(jnp.bfloat16), BLOCK)
        seed_rows = lax.dynamic_index_in_dim(init_index, group_id, 0, keepdims=False)
        centroids = own_rows[seed_rows].astype(jnp.float32)
        counts = jnp.zeros((K,), jnp.float32)
        for iteration in range(ITERS):
            weighted_totals, counts = responsibility_terms(candidate_rows, retained_rows, centroids, softness_scale)
            centroids = (weighted_totals + prior_weight * centroids) / (counts[:, None] + prior_weight)
        return centroids, counts

    centroids, counts = lax.map(one_group, jnp.arange(N_GROUP, dtype=jnp.int32))
    return centroids, counts
```

```python
from functools import partial

import jax
import jax.numpy as jnp
from jax import lax
from jax.experimental import pallas as pl
from jax.experimental.pallas import tpu as pltpu
from jax.sharding import PartitionSpec as P

ITERS = 2
PRIOR = 1.0
CORES = 2
TAIL = 8
BF16, F32 = jnp.bfloat16, jnp.float32
AXES = ("group", "sub")
VMEM = pl.BlockSpec(memory_space=pltpu.VMEM)
SMEM = pl.BlockSpec(memory_space=pltpu.SMEM)


def contract(a, b, dim_a, dim_b):
    return lax.dot_general(a, b, (((dim_a,), (dim_b,)), ((), ())), preferred_element_type=F32)


def column(row):
    k = row.shape[1]
    diagonal = lax.broadcasted_iota(jnp.int32, (k, k), 0) == lax.broadcasted_iota(jnp.int32, (k, k), 1)
    return jnp.sum(jnp.where(diagonal, row, jnp.zeros_like(row)), axis=1, keepdims=True)


def tree(terms):
    while len(terms) > 1:
        terms = [terms[i] + terms[i + 1] for i in range(0, len(terms), 2)]
    return terms[0]


def seed_kernel(index_ref, rows_ref, out_ref):
    rows = rows_ref.shape[0]
    picked = column(index_ref[...].astype(F32)).astype(jnp.int32) - lax.axis_index("sub") * rows
    onehot = (lax.broadcasted_iota(jnp.int32, (picked.shape[0], rows), 1) == picked).astype(F32).astype(BF16)
    out_ref[...] = contract(onehot, rows_ref[...], 1, 0).astype(BF16)


def accumulate(half, centroids, own_labels, other_labels, own_rows, other_rows, out_ref, sums, counts, block, scale):
    core = lax.rem(lax.axis_index("sub"), CORES)
    k, width = centroids.shape
    square = half.astype(F32)
    norms = jnp.sum(square * square, axis=1, keepdims=True)
    rows = own_rows.shape[0]
    step = rows
    first = True
    for labels, x_ref in ((own_labels, own_rows), (other_labels, other_rows)):
        for start in range(0, rows, step):
            x = x_ref[pl.ds(start, step), :]
            logits = (2.0 * contract(half, x, 1, 1) - norms) * (1.0 / scale)
            top = jnp.max(logits, axis=0, keepdims=True)
            e = jnp.exp(logits - top)
            weights = (e * (1.0 / jnp.sum(e, axis=0, keepdims=True))).astype(BF16)
            kept = jnp.concatenate(
                [
                    jnp.full((1, block), (labels[start // block + j] == core).astype(F32))
                    for j in range(step // block)
                ],
                axis=1,
            ).astype(BF16)
            weights = weights * kept
            part = contract(weights, x, 1, 0)
            number = contract(jnp.ones((TAIL, step), BF16), weights, 1, 1)
            if first:
                sums[...] = part
                counts[...] = number
            else:
                sums[...] += part
                counts[...] += number
            first = False
    out_ref[0:k, :] = sums[...].astype(BF16)
    number = counts[...]
    high = number.astype(BF16).astype(F32)
    line = lax.broadcasted_iota(jnp.int32, number.shape, 0)
    out_ref[k : k + TAIL, :] = jnp.zeros((TAIL, width), BF16)
    out_ref[k : k + TAIL, 0:k] = jnp.where(line == 0, high, number - high).astype(BF16)


def first_kernel(bit, block, scale, n, *refs):
    own_labels, other_labels, chip_ref = refs[:3]
    parts = refs[3 : 3 + n]
    own_rows, other_rows, out_ref, c_ref, sums, counts = refs[3 + n :]
    core = lax.rem(lax.axis_index("sub"), CORES)
    side = jnp.bitwise_and(jnp.right_shift(lax.axis_index("group"), bit), 1)
    chip = chip_ref[...].astype(F32)
    centroids = jnp.where(core == side, chip, jnp.zeros_like(chip))
    for part in parts:
        centroids = centroids + part[...].astype(F32)
    half = centroids.astype(BF16)
    c_ref[...] = half
    accumulate(half, centroids, own_labels, other_labels, own_rows, other_rows, out_ref, sums, counts, block, scale)


def updated(before, parts):
    k = before.shape[0]
    total = tree([part[0:k, :].astype(F32) for part in parts])
    tails = [part[k : k + TAIL, 0:k].astype(F32) for part in parts]
    number = tree([tail[0:1, :] + tail[1:2, :] for tail in tails])
    return (total + PRIOR * before) * (1.0 / (column(number) + PRIOR)), number


def next_kernel(block, scale, n, *refs):
    own_labels, other_labels, before_ref = refs[:3]
    parts = refs[3 : 3 + n]
    own_rows, other_rows, out_ref, c_ref, sums, counts = refs[3 + n :]
    centroids, _ = updated(before_ref[...].astype(F32), [part[...] for part in parts])
    c_ref[...] = centroids
    accumulate(
        centroids.astype(BF16), centroids, own_labels, other_labels, own_rows, other_rows, out_ref, sums, counts, block,
        scale,
    )


def last_kernel(n, *refs):
    before_ref, parts, out_ref = refs[0], refs[1 : 1 + n], refs[1 + n]
    k = before_ref.shape[0]
    centroids, number = updated(before_ref[...].astype(F32), [part[...] for part in parts])
    out_ref[0:k, :] = centroids
    out_ref[k : k + TAIL, :] = jnp.zeros((TAIL, out_ref.shape[1]), F32)
    out_ref[k : k + TAIL, 0:k] = jnp.broadcast_to(number, (TAIL, k))


def call(kernel, outs, scratch=(), smem=0, vmem=0, flops=0):
    return pl.pallas_call(
        kernel,
        out_shape=outs,
        in_specs=[SMEM] * smem + [VMEM] * vmem,
        out_specs=jax.tree.map(lambda _: VMEM, outs),
        scratch_shapes=list(scratch),
        compiler_params=pltpu.CompilerParams(vmem_limit_bytes=28 << 20),
        cost_estimate=pl.CostEstimate(flops=flops, bytes_accessed=1 << 20, transcendentals=0),
    )


class Plan:
    def __init__(self, bit):
        self.mask = 1 << bit
        self.groups = lax.axis_size("group")
        self.subs = lax.axis_size("sub")
        self.chips = self.subs // CORES
        self.bit = bit

    def devices(self):
        for group in range(self.groups):
            for sub in range(self.subs):
                yield group, sub // CORES, sub % CORES, (group >> self.bit) & 1

    def flat(self, group, chip, core):
        return group * self.subs + chip * CORES + core

    def seeds(self, value):
        received = []
        for step in range(self.chips):
            pairs = []
            for group, chip, core, side in self.devices():
                source = self.flat(group, chip, core)
                if core != side:
                    pairs.append((source, self.flat(group ^ self.mask, chip ^ step, 1 - core)))
                elif step:
                    pairs.append((source, self.flat(group, chip ^ step, core)))
            received.append(lax.ppermute(value, AXES, pairs))
        return received

    def sums(self, value, last):
        received = [value]
        for flip in (0, 1):
            for step in range(self.chips):
                if not flip and not step:
                    continue
                pairs = [
                    (self.flat(group, chip, core), self.flat(group ^ (self.mask * flip), chip ^ step, core))
                    for group, chip, core, side in self.devices()
                    if not last or core == side ^ flip
                ]
                received.append(lax.ppermute(value, AXES, pairs))
        return received


def swap_cores(value):
    return lax.ppermute(value, "sub", [(sub, sub ^ 1) for sub in range(lax.axis_size("sub"))])


def refine(chip_seeds, own_labels, other_labels, own_rows, other_rows, bit):
    plan = Plan(bit)
    k, width = chip_seeds.shape
    rows = own_rows.shape[0]
    block = rows // own_labels.shape[0]
    scale = width / 8.0
    payload = jax.ShapeDtypeStruct((k + TAIL, width), BF16)
    scratch = [pltpu.VMEM((k, width), F32), pltpu.VMEM((TAIL, k), F32)]
    flops = 8 * rows * k * width

    seeds = plan.seeds(chip_seeds)
    parts, centroids = call(
        partial(first_kernel, bit, block, scale, len(seeds)),
        (payload, jax.ShapeDtypeStruct((k, width), BF16)),
        scratch, 2, 3 + len(seeds), flops,
    )(own_labels, other_labels, chip_seeds, *seeds, own_rows, other_rows)
    for _ in range(ITERS - 1):
        shares = plan.sums(parts, False)
        parts, centroids = call(
            partial(next_kernel, block, scale, len(shares)),
            (payload, jax.ShapeDtypeStruct((k, width), F32)),
            scratch, 2, 3 + len(shares), flops,
        )(own_labels, other_labels, centroids, *shares, own_rows, other_rows)
    shares = plan.sums(parts, True)
    mine = call(
        partial(last_kernel, len(shares)), jax.ShapeDtypeStruct((k + TAIL, width), F32), (), 0, 1 + len(shares)
    )(centroids, *shares)
    theirs = swap_cores(mine)
    core = lax.rem(lax.axis_index("sub"), CORES)
    side = jnp.bitwise_and(jnp.right_shift(lax.axis_index("group"), bit), 1)
    result = jnp.where(core == side, mine, theirs)
    return result[None, 0:k], result[k : k + 1, 0:k]


def local(embeddings, labels, group_bit, init_index):
    k, width = init_index.shape[1], embeddings.shape[1]
    levels = lax.axis_size("group").bit_length() - 1
    seeds = call(seed_kernel, jax.ShapeDtypeStruct((k, width), BF16), (), 0, 2)(init_index, embeddings)
    chip_seeds = seeds + swap_cores(seeds)
    other_labels = swap_cores(labels)
    other_rows = swap_cores(embeddings)
    return lax.switch(
        group_bit[0],
        [partial(refine, bit=bit) for bit in range(levels)],
        chip_seeds, labels, other_labels, embeddings, other_rows,
    )


def solution(mesh):
    return jax.shard_map(
        local,
        mesh=mesh,
        in_specs=(P(("group", "sub"), None), P(("group", "sub")), P(), P("group", None)),
        out_specs=(P("group", None, None), P("group", None)),
        check_vma=False,
    )
```

```python
from functools import partial

import jax
import jax.numpy as jnp
from jax import lax
from jax.experimental import pallas as pl
from jax.experimental.pallas import tpu as pltpu
from jax.sharding import PartitionSpec as P

ITERS = 2
PRIOR = 1.0
CORES = 2
TAIL = 8
LANES = 128
CHUNKS = 4
FAR = 2
BF16, F32 = jnp.bfloat16, jnp.float32
AXES = ("group", "sub")
VMEM = pl.BlockSpec(memory_space=pltpu.VMEM)
SMEM = pl.BlockSpec(memory_space=pltpu.SMEM)
HBM = pl.BlockSpec(memory_space=pltpu.HBM)


def contract(a, b, dim_a, dim_b):
    return lax.dot_general(a, b, (((dim_a,), (dim_b,)), ((), ())), preferred_element_type=F32)


def column(row):
    k = row.shape[1]
    diagonal = lax.broadcasted_iota(jnp.int32, (k, k), 0) == lax.broadcasted_iota(jnp.int32, (k, k), 1)
    return jnp.sum(jnp.where(diagonal, row, jnp.zeros_like(row)), axis=1, keepdims=True)


def halves(number):
    high = number.astype(BF16).astype(F32)
    return jnp.where(lax.broadcasted_iota(jnp.int32, number.shape, 0) == 0, high, number - high).astype(BF16)


def tree(terms):
    while len(terms) > 1:
        terms = [terms[i] + terms[i + 1] for i in range(0, len(terms), 2)]
    return terms[0]


def seed_kernel(index_ref, labels_ref, rows_ref, out_ref, held_ref, index, sems):
    chunks = sems.shape[0] - 1
    k, width = index_ref.shape[1], rows_ref.shape[1]
    rows = rows_ref.shape[0]
    size = rows // chunks
    first = pltpu.make_async_copy(index_ref, index, sems.at[chunks])
    first.start()
    copies = []
    for i in range(chunks):
        span = pl.ds(i * size, size)
        copies.append(pltpu.make_async_copy(rows_ref.at[span], held_ref.at[span], sems.at[i]))
        copies[-1].start()
    first.wait()
    picked = column(index[...].astype(F32)).astype(jnp.int32) - lax.axis_index("sub") * rows
    total = jnp.zeros((k, width), F32)
    for i in range(chunks):
        onehot = (lax.broadcasted_iota(jnp.int32, (k, size), 1) == picked - i * size).astype(F32).astype(BF16)
        copies[i].wait()
        total = total + contract(onehot, held_ref[pl.ds(i * size, size), :], 1, 0)
    out_ref[0:k, :] = total.astype(BF16)
    out_ref[k : k + TAIL, :] = jnp.zeros((TAIL, width), BF16)
    blocks = labels_ref.shape[0]
    lane = lax.broadcasted_iota(jnp.int32, (TAIL, LANES), 1)
    marks = jnp.zeros((TAIL, LANES), F32)
    for j in range(blocks):
        marks = jnp.where(lane == j, labels_ref[j].astype(F32), marks)
    out_ref[k : k + TAIL, 0:LANES] = marks.astype(BF16)


def accumulate(half, own_marks, other_marks, own_rows, other_rows, out_ref, sums, counts, block, scale):
    core = lax.rem(lax.axis_index("sub"), CORES)
    k, width = half.shape
    square = half.astype(F32)
    norms = jnp.sum(square * square, axis=1, keepdims=True)
    rows = own_rows.shape[0]
    step = rows
    first = True
    for marks, x_ref in ((own_marks, own_rows), (other_marks, other_rows)):
        kept_marks = (marks[k : k + 1, 0:LANES].astype(F32) == core.astype(F32)).astype(F32)
        for start in range(0, rows, step):
            x = x_ref[pl.ds(start, step), :]
            logits = (2.0 * contract(half, x, 1, 1) - norms) * (1.0 / scale)
            top = jnp.max(logits, axis=0, keepdims=True)
            e = jnp.exp(logits - top)
            weights = (e * (1.0 / jnp.sum(e, axis=0, keepdims=True))).astype(BF16)
            kept = jnp.concatenate(
                [
                    jnp.broadcast_to(kept_marks[:, start // block + j : start // block + j + 1], (1, block))
                    for j in range(step // block)
                ],
                axis=1,
            ).astype(BF16)
            weights = weights * kept
            part = contract(weights, x, 1, 0)
            number = contract(jnp.ones((TAIL, step), BF16), weights, 1, 1)
            if first:
                sums[...] = part
                counts[...] = number
            else:
                sums[...] += part
                counts[...] += number
            first = False
    out_ref[0:k, :] = sums[...].astype(BF16)
    out_ref[k : k + TAIL, :] = jnp.zeros((TAIL, width), BF16)
    out_ref[k : k + TAIL, 0:k] = halves(counts[...])


def first_kernel(bit, block, scale, n, *refs):
    own_marks, other_marks = refs[:2]
    parts = refs[2 : 2 + n]
    own_rows, other_rows, out_ref, c_ref, sums, counts = refs[2 + n :]
    core = lax.rem(lax.axis_index("sub"), CORES)
    side = jnp.bitwise_and(jnp.right_shift(lax.axis_index("group"), bit), 1)
    k = c_ref.shape[0]
    chip = own_marks[0:k, :].astype(F32) + other_marks[0:k, :].astype(F32)
    near = parts[0][0:k, :].astype(F32)
    centroids = jnp.where(core == side, chip, near)
    for part in parts[1:]:
        centroids = centroids + part[0:k, :].astype(F32)
    half = centroids.astype(BF16)
    c_ref[...] = half
    accumulate(half, own_marks, other_marks, own_rows, other_rows, out_ref, sums, counts, block, scale)


def updated(before, parts):
    k = before.shape[0]
    total = tree([part[0:k, :].astype(F32) for part in parts])
    tails = [part[k : k + TAIL, 0:k].astype(F32) for part in parts]
    number = tree([tail[0:1, :] + tail[1:2, :] for tail in tails])
    return (total + PRIOR * before) * (1.0 / (column(number) + PRIOR)), number


def next_kernel(block, scale, n, *refs):
    own_marks, other_marks, before_ref = refs[:3]
    parts = refs[3 : 3 + n]
    own_rows, other_rows, out_ref, c_ref, sums, counts = refs[3 + n :]
    centroids, _ = updated(before_ref[...].astype(F32), [part[...] for part in parts])
    c_ref[...] = centroids
    accumulate(
        centroids.astype(BF16), own_marks, other_marks, own_rows, other_rows, out_ref, sums, counts, block, scale
    )


def merge_kernel(own_ref, other_ref, out_ref):
    k = own_ref.shape[0] - TAIL
    out_ref[0:k, :] = (own_ref[0:k, :].astype(F32) + other_ref[0:k, :].astype(F32)).astype(BF16)
    tail = own_ref[k : k + TAIL, :].astype(F32) + other_ref[k : k + TAIL, :].astype(F32)
    number = jnp.broadcast_to(tail[0:1, :] + tail[1:2, :], tail.shape)
    out_ref[k : k + TAIL, :] = halves(number)


def last_kernel(n, *refs):
    before_ref, parts, out_ref = refs[0], refs[1 : 1 + n], refs[1 + n]
    k = before_ref.shape[0]
    centroids, number = updated(before_ref[...].astype(F32), [part[...] for part in parts])
    out_ref[0:k, :] = centroids
    out_ref[k : k + TAIL, :] = jnp.zeros((TAIL, out_ref.shape[1]), F32)
    out_ref[k : k + TAIL, 0:k] = jnp.broadcast_to(number, (TAIL, k))


def output_kernel(bit, mine_ref, theirs_ref, out_ref, number_ref, sems):
    k = out_ref.shape[1]
    core = lax.rem(lax.axis_index("sub"), CORES)
    side = jnp.bitwise_and(jnp.right_shift(lax.axis_index("group"), bit), 1)

    def write(source):
        copy = pltpu.make_async_copy(source.at[0:k], out_ref.at[0], sems.at[0])
        copy.start()
        number_ref[...] = source[k : k + 1, 0:k]
        copy.wait()

    @pl.when(core == side)
    def _():
        write(mine_ref)

    @pl.when(core != side)
    def _():
        write(theirs_ref)


def call(kernel, ins, outs, out_specs=VMEM, scratch=(), flops=0):
    return pl.pallas_call(
        kernel,
        out_shape=outs,
        in_specs=ins,
        out_specs=out_specs,
        scratch_shapes=list(scratch),
        compiler_params=pltpu.CompilerParams(vmem_limit_bytes=28 << 20),
        cost_estimate=pl.CostEstimate(flops=flops, bytes_accessed=1 << 20, transcendentals=0),
    )


class Plan:
    def __init__(self, bit):
        self.mask = 1 << bit
        self.groups = lax.axis_size("group")
        self.subs = lax.axis_size("sub")
        self.chips = self.subs // CORES
        self.bit = bit

    def devices(self):
        for group in range(self.groups):
            for sub in range(self.subs):
                yield group, sub // CORES, sub % CORES, (group >> self.bit) & 1

    def flat(self, group, chip, core):
        return group * self.subs + chip * CORES + core

    def permute(self, value, target):
        pairs = [(self.flat(*device[:3]), self.flat(*target(*device))) for device in self.devices()]
        return lax.ppermute(value, AXES, pairs)

    def seeds(self, value):
        received = []
        for step in range(self.chips):

            def target(group, chip, core, side):
                if step:
                    return (group, chip ^ step, core) if core == side else (group ^ self.mask, chip ^ step, 1 - core)
                return (group ^ self.mask, chip, core) if core == side else (group, chip, 1 - core)

            received.append(self.permute(value, target))
        return received

    def sums(self, value):
        received = [value]
        if self.bit >= FAR:
            step = 1
            while step < self.chips:
                received = [value, self.permute(value, lambda group, chip, core, side: (group, chip ^ step, core))]
                value = merge(*received)
                step *= 2
            return [value, self.permute(value, lambda group, chip, core, side: (group ^ self.mask, chip, core))]
        for flip in (0, 1):
            for step in range(self.chips):
                if flip or step:
                    received.append(
                        self.permute(
                            value,
                            lambda group, chip, core, side: (group ^ (self.mask * flip), chip ^ step, core),
                        )
                    )
        return received

    def last_sums(self, value):
        received = [value]
        for step in range(1, self.chips):
            received.append(self.permute(value, lambda group, chip, core, side: (group, chip ^ step, core)))
        for step in range(self.chips):
            received.append(
                self.permute(
                    value,
                    lambda group, chip, core, side: (
                        (group, chip, 1 - core) if core == side else (group ^ self.mask, chip ^ step, core)
                    ),
                )
            )
        return received


def merge(own, other):
    return call(merge_kernel, [VMEM] * 2, jax.ShapeDtypeStruct(own.shape, own.dtype))(own, other)


def swap_cores(value):
    return lax.ppermute(value, "sub", [(sub, sub ^ 1) for sub in range(lax.axis_size("sub"))])


def refine(own_marks, other_marks, own_rows, other_rows, bit, block):
    plan = Plan(bit)
    k, width = own_marks.shape[0] - TAIL, own_marks.shape[1]
    rows = own_rows.shape[0]
    scale = width / 8.0
    payload = jax.ShapeDtypeStruct((k + TAIL, width), BF16)
    scratch = [pltpu.VMEM((k, width), F32), pltpu.VMEM((TAIL, k), F32)]
    flops = 8 * rows * k * width

    seeds = plan.seeds(own_marks + other_marks)
    parts, centroids = call(
        partial(first_kernel, bit, block, scale, len(seeds)),
        [VMEM] * (4 + len(seeds)), (payload, jax.ShapeDtypeStruct((k, width), BF16)), (VMEM, VMEM), scratch, flops,
    )(own_marks, other_marks, *seeds, own_rows, other_rows)
    for _ in range(ITERS - 1):
        shares = plan.sums(parts)
        parts, centroids = call(
            partial(next_kernel, block, scale, len(shares)),
            [VMEM] * (5 + len(shares)), (payload, jax.ShapeDtypeStruct((k, width), F32)), (VMEM, VMEM), scratch, flops,
        )(own_marks, other_marks, centroids, *shares, own_rows, other_rows)
    shares = plan.last_sums(parts)
    mine = call(
        partial(last_kernel, len(shares)), [VMEM] * (1 + len(shares)), jax.ShapeDtypeStruct((k + TAIL, width), F32)
    )(centroids, *shares)
    return call(
        partial(output_kernel, bit), [VMEM] * 2,
        (jax.ShapeDtypeStruct((1, k, width), F32), jax.ShapeDtypeStruct((1, k), F32)), (HBM, VMEM),
        [pltpu.SemaphoreType.DMA((1,))],
    )(mine, swap_cores(mine))


def local(embeddings, labels, group_bit, init_index):
    k, width = init_index.shape[1], embeddings.shape[1]
    rows = embeddings.shape[0]
    levels = lax.axis_size("group").bit_length() - 1
    own_marks, own_rows = call(
        seed_kernel, [HBM, SMEM, HBM],
        (jax.ShapeDtypeStruct((k + TAIL, width), BF16), jax.ShapeDtypeStruct((rows, width), BF16)), (VMEM, VMEM),
        [pltpu.VMEM((1, k), jnp.int32), pltpu.SemaphoreType.DMA((CHUNKS + 1,))], 2 * k * rows * width,
    )(init_index, labels, embeddings)
    other_marks = swap_cores(own_marks)
    other_rows = swap_cores(own_rows)
    block = rows // labels.shape[0]
    return lax.switch(
        group_bit[0],
        [partial(refine, bit=bit, block=block) for bit in range(levels)],
        own_marks, other_marks, own_rows, other_rows,
    )


def solution(mesh):
    return jax.shard_map(
        local,
        mesh=mesh,
        in_specs=(P(("group", "sub"), None), P(("group", "sub")), P(), P("group", None)),
        out_specs=(P("group", None, None), P("group", None)),
        check_vma=False,
    )
```

```python
from functools import partial

import jax
import jax.numpy as jnp
from jax import lax
from jax.experimental import pallas as pl
from jax.experimental.pallas import tpu as pltpu
from jax.sharding import PartitionSpec as P

ITERS = 2
PRIOR = 1.0
CORES = 2
TAIL = 8
LANES = 128
SEED_VMEM = 60 << 20
CHUNKS = 4
FAR = 2
BF16, F32 = jnp.bfloat16, jnp.float32
AXES = ("group", "sub")
VMEM = pl.BlockSpec(memory_space=pltpu.VMEM)
SMEM = pl.BlockSpec(memory_space=pltpu.SMEM)
HBM = pl.BlockSpec(memory_space=pltpu.HBM)


def contract(a, b, dim_a, dim_b):
    return lax.dot_general(a, b, (((dim_a,), (dim_b,)), ((), ())), preferred_element_type=F32)


def column(row):
    k = row.shape[1]
    diagonal = lax.broadcasted_iota(jnp.int32, (k, k), 0) == lax.broadcasted_iota(jnp.int32, (k, k), 1)
    return jnp.sum(jnp.where(diagonal, row, jnp.zeros_like(row)), axis=1, keepdims=True)


def halves(number):
    high = number.astype(BF16).astype(F32)
    return jnp.where(lax.broadcasted_iota(jnp.int32, number.shape, 0) == 0, high, number - high).astype(BF16)


def tree(terms):
    while len(terms) > 1:
        terms = [terms[i] + terms[i + 1] for i in range(0, len(terms), 2)]
    return terms[0]


def seed_kernel(index_ref, labels_ref, rows_ref, out_ref, held_ref, index, sems):
    chunks = sems.shape[0] - 1
    k, width = index_ref.shape[1], rows_ref.shape[1]
    rows = rows_ref.shape[0]
    size = rows // chunks
    first = pltpu.make_async_copy(index_ref, index, sems.at[chunks])
    first.start()
    copies = []
    for i in range(chunks):
        span = pl.ds(i * size, size)
        copies.append(pltpu.make_async_copy(rows_ref.at[span], held_ref.at[span], sems.at[i]))
        copies[-1].start()
    first.wait()
    picked = column(index[...].astype(F32)).astype(jnp.int32) - lax.axis_index("sub") * rows
    total = jnp.zeros((k, width), F32)
    for i in range(chunks):
        onehot = (lax.broadcasted_iota(jnp.int32, (k, size), 1) == picked - i * size).astype(F32).astype(BF16)
        copies[i].wait()
        total = total + contract(onehot, held_ref[pl.ds(i * size, size), :], 1, 0)
    out_ref[0:k, :] = total.astype(BF16)
    out_ref[k : k + TAIL, :] = jnp.zeros((TAIL, width), BF16)
    blocks = labels_ref.shape[0]
    lane = lax.broadcasted_iota(jnp.int32, (TAIL, LANES), 1)
    marks = jnp.zeros((TAIL, LANES), F32)
    for j in range(blocks):
        marks = jnp.where(lane == j, labels_ref[j].astype(F32), marks)
    out_ref[k : k + TAIL, 0:LANES] = marks.astype(BF16)


def accumulate(half, own_marks, other_marks, own_rows, other_rows, out_ref, sums, counts, block, scale):
    core = lax.rem(lax.axis_index("sub"), CORES)
    k, width = half.shape
    square = half.astype(F32)
    norms = jnp.sum(square * square, axis=1, keepdims=True)
    rows = own_rows.shape[0]
    step = rows
    first = True
    for marks, x_ref in ((own_marks, own_rows), (other_marks, other_rows)):
        kept_marks = (marks[k : k + 1, 0:LANES].astype(F32) == core.astype(F32)).astype(F32)
        for start in range(0, rows, step):
            x = x_ref[pl.ds(start, step), :]
            logits = (2.0 * contract(half, x, 1, 1) - norms) * (1.0 / scale)
            top = jnp.max(logits, axis=0, keepdims=True)
            e = jnp.exp(logits - top)
            weights = (e * (1.0 / jnp.sum(e, axis=0, keepdims=True))).astype(BF16)
            kept = jnp.concatenate(
                [
                    jnp.broadcast_to(kept_marks[:, start // block + j : start // block + j + 1], (1, block))
                    for j in range(step // block)
                ],
                axis=1,
            ).astype(BF16)
            weights = weights * kept
            part = contract(weights, x, 1, 0)
            number = contract(jnp.ones((TAIL, step), BF16), weights, 1, 1)
            if first:
                sums[...] = part
                counts[...] = number
            else:
                sums[...] += part
                counts[...] += number
            first = False
    out_ref[0:k, :] = sums[...].astype(BF16)
    out_ref[k : k + TAIL, :] = jnp.zeros((TAIL, width), BF16)
    out_ref[k : k + TAIL, 0:k] = halves(counts[...])


def first_kernel(bit, block, scale, n, *refs):
    own_marks, other_marks = refs[:2]
    parts = refs[2 : 2 + n]
    own_rows, other_rows, out_ref, c_ref, sums, counts = refs[2 + n :]
    core = lax.rem(lax.axis_index("sub"), CORES)
    side = jnp.bitwise_and(jnp.right_shift(lax.axis_index("group"), bit), 1)
    k = c_ref.shape[0]
    chip = own_marks[0:k, :].astype(F32) + other_marks[0:k, :].astype(F32)
    near = parts[0][0:k, :].astype(F32)
    centroids = jnp.where(core == side, chip, near)
    for part in parts[1:]:
        centroids = centroids + part[0:k, :].astype(F32)
    half = centroids.astype(BF16)
    c_ref[...] = half
    accumulate(half, own_marks, other_marks, own_rows, other_rows, out_ref, sums, counts, block, scale)


def updated(before, parts):
    k = before.shape[0]
    total = tree([part[0:k, :].astype(F32) for part in parts])
    tails = [part[k : k + TAIL, 0:k].astype(F32) for part in parts]
    number = tree([tail[0:1, :] + tail[1:2, :] for tail in tails])
    return (total + PRIOR * before) * (1.0 / (column(number) + PRIOR)), number


def next_kernel(block, scale, n, *refs):
    own_marks, other_marks, before_ref = refs[:3]
    parts = refs[3 : 3 + n]
    own_rows, other_rows, out_ref, c_ref, sums, counts = refs[3 + n :]
    centroids, _ = updated(before_ref[...].astype(F32), [part[...] for part in parts])
    c_ref[...] = centroids
    accumulate(
        centroids.astype(BF16), own_marks, other_marks, own_rows, other_rows, out_ref, sums, counts, block, scale
    )


def merge_kernel(own_ref, other_ref, out_ref):
    k = own_ref.shape[0] - TAIL
    out_ref[0:k, :] = (own_ref[0:k, :].astype(F32) + other_ref[0:k, :].astype(F32)).astype(BF16)
    tail = own_ref[k : k + TAIL, :].astype(F32) + other_ref[k : k + TAIL, :].astype(F32)
    number = jnp.broadcast_to(tail[0:1, :] + tail[1:2, :], tail.shape)
    out_ref[k : k + TAIL, :] = halves(number)


def last_kernel(n, *refs):
    before_ref, parts, out_ref = refs[0], refs[1 : 1 + n], refs[1 + n]
    k = before_ref.shape[0]
    centroids, number = updated(before_ref[...].astype(F32), [part[...] for part in parts])
    out_ref[0:k, :] = centroids
    out_ref[k : k + TAIL, :] = jnp.zeros((TAIL, out_ref.shape[1]), F32)
    out_ref[k : k + TAIL, 0:k] = jnp.broadcast_to(number, (TAIL, k))


def output_kernel(bit, mine_ref, theirs_ref, out_ref, number_ref, sems):
    k = out_ref.shape[1]
    core = lax.rem(lax.axis_index("sub"), CORES)
    side = jnp.bitwise_and(jnp.right_shift(lax.axis_index("group"), bit), 1)

    def write(source):
        copy = pltpu.make_async_copy(source.at[0:k], out_ref.at[0], sems.at[0])
        copy.start()
        number_ref[...] = source[k : k + 1, 0:k]
        copy.wait()

    @pl.when(core == side)
    def _():
        write(mine_ref)

    @pl.when(core != side)
    def _():
        write(theirs_ref)


def call(kernel, ins, outs, out_specs=VMEM, scratch=(), flops=0, limit=28 << 20):
    return pl.pallas_call(
        kernel,
        out_shape=outs,
        in_specs=ins,
        out_specs=out_specs,
        scratch_shapes=list(scratch),
        compiler_params=pltpu.CompilerParams(vmem_limit_bytes=limit),
        cost_estimate=pl.CostEstimate(flops=flops, bytes_accessed=1 << 20, transcendentals=0),
    )


class Plan:
    def __init__(self, bit):
        self.mask = 1 << bit
        self.groups = lax.axis_size("group")
        self.subs = lax.axis_size("sub")
        self.chips = self.subs // CORES
        self.bit = bit

    def devices(self):
        for group in range(self.groups):
            for sub in range(self.subs):
                yield group, sub // CORES, sub % CORES, (group >> self.bit) & 1

    def flat(self, group, chip, core):
        return group * self.subs + chip * CORES + core

    def permute(self, value, target):
        pairs = [(self.flat(*device[:3]), self.flat(*target(*device))) for device in self.devices()]
        return lax.ppermute(value, AXES, pairs)

    def seeds(self, value):
        received = []
        for step in range(self.chips):

            def target(group, chip, core, side):
                if step:
                    return (group, chip ^ step, core) if core == side else (group ^ self.mask, chip ^ step, 1 - core)
                return (group ^ self.mask, chip, core) if core == side else (group, chip, 1 - core)

            received.append(self.permute(value, target))
        return received

    def sums(self, value):
        received = [value]
        if self.bit >= FAR:
            step = 1
            while step < self.chips:
                received = [value, self.permute(value, lambda group, chip, core, side: (group, chip ^ step, core))]
                value = merge(*received)
                step *= 2
            return [value, self.permute(value, lambda group, chip, core, side: (group ^ self.mask, chip, core))]
        for flip in (0, 1):
            for step in range(self.chips):
                if flip or step:
                    received.append(
                        self.permute(
                            value,
                            lambda group, chip, core, side: (group ^ (self.mask * flip), chip ^ step, core),
                        )
                    )
        return received

    def last_sums(self, value):
        received = [value]
        for step in range(1, self.chips):
            received.append(self.permute(value, lambda group, chip, core, side: (group, chip ^ step, core)))
        for step in range(self.chips):
            received.append(
                self.permute(
                    value,
                    lambda group, chip, core, side: (
                        (group, chip, 1 - core) if core == side else (group ^ self.mask, chip ^ step, core)
                    ),
                )
            )
        return received


def merge(own, other):
    return call(merge_kernel, [VMEM] * 2, jax.ShapeDtypeStruct(own.shape, own.dtype))(own, other)


def swap_cores(value):
    return lax.ppermute(value, "sub", [(sub, sub ^ 1) for sub in range(lax.axis_size("sub"))])


def refine(own_marks, other_marks, own_rows, bit, block):
    plan = Plan(bit)
    other_rows = swap_cores(own_rows)
    k, width = own_marks.shape[0] - TAIL, own_marks.shape[1]
    rows = own_rows.shape[0]
    scale = width / 8.0
    payload = jax.ShapeDtypeStruct((k + TAIL, width), BF16)
    scratch = [pltpu.VMEM((k, width), F32), pltpu.VMEM((TAIL, k), F32)]
    flops = 8 * rows * k * width

    seeds = plan.seeds(own_marks + other_marks)
    parts, centroids = call(
        partial(first_kernel, bit, block, scale, len(seeds)),
        [VMEM] * (4 + len(seeds)), (payload, jax.ShapeDtypeStruct((k, width), BF16)), (VMEM, VMEM), scratch, flops,
    )(own_marks, other_marks, *seeds, own_rows, other_rows)
    for _ in range(ITERS - 1):
        shares = plan.sums(parts)
        parts, centroids = call(
            partial(next_kernel, block, scale, len(shares)),
            [VMEM] * (5 + len(shares)), (payload, jax.ShapeDtypeStruct((k, width), F32)), (VMEM, VMEM), scratch, flops,
        )(own_marks, other_marks, centroids, *shares, own_rows, other_rows)
    shares = plan.last_sums(parts)
    mine = call(
        partial(last_kernel, len(shares)), [VMEM] * (1 + len(shares)), jax.ShapeDtypeStruct((k + TAIL, width), F32)
    )(centroids, *shares)
    return call(
        partial(output_kernel, bit), [VMEM] * 2,
        (jax.ShapeDtypeStruct((1, k, width), F32), jax.ShapeDtypeStruct((1, k), F32)), (HBM, VMEM),
        [pltpu.SemaphoreType.DMA((1,))],
    )(mine, swap_cores(mine))


def local(embeddings, labels, group_bit, init_index):
    k, width = init_index.shape[1], embeddings.shape[1]
    rows = embeddings.shape[0]
    levels = lax.axis_size("group").bit_length() - 1
    own_marks, own_rows = call(
        seed_kernel, [HBM, SMEM, HBM],
        (jax.ShapeDtypeStruct((k + TAIL, width), BF16), jax.ShapeDtypeStruct((rows, width), BF16)), (VMEM, VMEM),
        [pltpu.VMEM((1, k), jnp.int32), pltpu.SemaphoreType.DMA((CHUNKS + 1,))], 2 * k * rows * width, SEED_VMEM,
    )(init_index, labels, embeddings)
    other_marks = swap_cores(own_marks)
    block = rows // labels.shape[0]
    return lax.switch(
        group_bit[0],
        [partial(refine, bit=bit, block=block) for bit in range(levels)],
        own_marks, other_marks, own_rows,
    )


def solution(mesh):
    return jax.shard_map(
        local,
        mesh=mesh,
        in_specs=(P(("group", "sub"), None), P(("group", "sub")), P(), P("group", None)),
        out_specs=(P("group", None, None), P("group", None)),
        check_vma=False,
    )
```

```python
from functools import partial

import jax
import jax.numpy as jnp
from jax import lax
from jax.experimental import pallas as pl
from jax.experimental.pallas import tpu as pltpu
from jax.sharding import PartitionSpec as P

ITERS = 2
PRIOR = 1.0
CORES = 2
TAIL = 8
LANES = 128
SEED_VMEM = 60 << 20
CHUNKS = 4
FAR = 2
BF16, F32 = jnp.bfloat16, jnp.float32
AXES = ("group", "sub")
VMEM = pl.BlockSpec(memory_space=pltpu.VMEM)
HBM = pl.BlockSpec(memory_space=pltpu.HBM)


def contract(a, b, dim_a, dim_b):
    return lax.dot_general(a, b, (((dim_a,), (dim_b,)), ((), ())), preferred_element_type=F32)


def column(row):
    k = row.shape[1]
    diagonal = lax.broadcasted_iota(jnp.int32, (k, k), 0) == lax.broadcasted_iota(jnp.int32, (k, k), 1)
    return jnp.sum(jnp.where(diagonal, row, jnp.zeros_like(row)), axis=1, keepdims=True)


def halves(number):
    high = number.astype(BF16).astype(F32)
    return jnp.where(lax.broadcasted_iota(jnp.int32, number.shape, 0) == 0, high, number - high).astype(BF16)


def tree(terms):
    while len(terms) > 1:
        terms = [terms[i] + terms[i + 1] for i in range(0, len(terms), 2)]
    return terms[0]


def seed_kernel(index_ref, labels_ref, rows_ref, out_ref, held_ref, index, labels, sems):
    chunks = sems.shape[0] - 2
    k, width = index_ref.shape[1], rows_ref.shape[1]
    rows = rows_ref.shape[0]
    size = rows // chunks
    first = pltpu.make_async_copy(index_ref, index, sems.at[chunks])
    first.start()
    second = pltpu.make_async_copy(labels_ref, labels, sems.at[chunks + 1])
    second.start()
    copies = []
    for i in range(chunks):
        span = pl.ds(i * size, size)
        copies.append(pltpu.make_async_copy(rows_ref.at[span], held_ref.at[span], sems.at[i]))
        copies[-1].start()
    first.wait()
    picked = column(index[...].astype(F32)).astype(jnp.int32) - lax.axis_index("sub") * rows
    total = jnp.zeros((k, width), F32)
    for i in range(chunks):
        onehot = (lax.broadcasted_iota(jnp.int32, (k, size), 1) == picked - i * size).astype(F32).astype(BF16)
        copies[i].wait()
        total = total + contract(onehot, held_ref[pl.ds(i * size, size), :], 1, 0)
    out_ref[0:k, :] = total.astype(BF16)
    out_ref[k : k + TAIL, :] = jnp.zeros((TAIL, width), BF16)
    second.wait()
    marks = jnp.concatenate([labels[...].astype(F32), jnp.zeros((1, LANES - labels.shape[1]), F32)], axis=1)
    out_ref[k : k + TAIL, 0:LANES] = jnp.broadcast_to(marks, (TAIL, LANES)).astype(BF16)


def turn_kernel(rows_ref, out_ref):
    out_ref[...] = rows_ref[...].T


def accumulate(half, own, other, out_refs, sums, counts, block, scale):
    core = lax.rem(lax.axis_index("sub"), CORES)
    k, width = half.shape
    square = half.astype(F32)
    norms = jnp.sum(square * square, axis=1, keepdims=True)
    for first, (marks, rows_ref, turned_ref) in ((True, own), (False, other)):
        rows = rows_ref.shape[0]
        kept_marks = (marks[k : k + 1, 0:LANES].astype(F32) == core.astype(F32)).astype(F32)
        logits = (2.0 * contract(half, turned_ref[...], 1, 0) - norms) * (1.0 / scale)
        top = jnp.max(logits, axis=0, keepdims=True)
        e = jnp.exp(logits - top)
        weights = (e * (1.0 / jnp.sum(e, axis=0, keepdims=True))).astype(BF16)
        kept = jnp.concatenate(
            [jnp.broadcast_to(kept_marks[:, j : j + 1], (1, block)) for j in range(rows // block)], axis=1
        ).astype(BF16)
        weights = weights * kept
        part = contract(weights, rows_ref[...], 1, 0)
        number = contract(jnp.ones((TAIL, rows), BF16), weights, 1, 1)
        if first:
            sums[...] = part
            counts[...] = number
        else:
            sums[...] += part
            counts[...] += number
    size = k // len(out_refs)
    for i, out_ref in enumerate(out_refs):
        out_ref[0:size, :] = sums[i * size : (i + 1) * size, :].astype(BF16)
        out_ref[size : size + TAIL, :] = jnp.zeros((TAIL, width), BF16)
        out_ref[size : size + TAIL, 0:k] = halves(counts[...])


def first_kernel(bit, block, scale, n, far, *refs):
    own_marks, other_marks = refs[:2]
    parts = refs[2 : 2 + n]
    own_rows, other_rows, own_turned, other_turned = refs[2 + n : 6 + n]
    out_refs, (c_ref, sums, counts) = refs[6 + n : -3], refs[-3:]
    core = lax.rem(lax.axis_index("sub"), CORES)
    side = jnp.bitwise_and(jnp.right_shift(lax.axis_index("group"), bit), 1)
    k = c_ref.shape[0]
    if far:
        chip = parts[1][0:k, :].astype(F32)
    else:
        chip = own_marks[0:k, :].astype(F32) + other_marks[0:k, :].astype(F32)
    centroids = jnp.where(core == side, chip, parts[0][0:k, :].astype(F32))
    if not far:
        for part in parts[1:]:
            centroids = centroids + part[0:k, :].astype(F32)
    half = centroids.astype(BF16)
    c_ref[...] = half
    accumulate(
        half, (own_marks, own_rows, own_turned), (other_marks, other_rows, other_turned), out_refs, sums, counts,
        block, scale,
    )


def updated(before, pieces):
    k = before.shape[0]
    size = k // len(pieces)
    total = jnp.concatenate([tree([part[0:size, :].astype(F32) for part in parts]) for parts in pieces], axis=0)
    tails = [part[size : size + TAIL, 0:k].astype(F32) for part in pieces[0]]
    number = tree([tail[0:1, :] + tail[1:2, :] for tail in tails])
    return (total + PRIOR * before) * (1.0 / (column(number) + PRIOR)), number


def split(refs, pieces):
    each = len(refs) // pieces
    return [[ref[...] for ref in refs[i * each : (i + 1) * each]] for i in range(pieces)]


def next_kernel(block, scale, n, pieces, *refs):
    own_marks, other_marks, before_ref = refs[:3]
    parts = refs[3 : 3 + n]
    own_rows, other_rows, own_turned, other_turned = refs[3 + n : 7 + n]
    out_refs, (c_ref, sums, counts) = refs[7 + n : -3], refs[-3:]
    centroids, _ = updated(before_ref[...].astype(F32), split(parts, pieces))
    c_ref[...] = centroids
    accumulate(
        centroids.astype(BF16), (own_marks, own_rows, own_turned), (other_marks, other_rows, other_turned), out_refs,
        sums, counts, block, scale,
    )


def merge_kernel(own_ref, other_ref, out_ref):
    k = own_ref.shape[0] - TAIL
    out_ref[0:k, :] = (own_ref[0:k, :].astype(F32) + other_ref[0:k, :].astype(F32)).astype(BF16)
    tail = own_ref[k : k + TAIL, :].astype(F32) + other_ref[k : k + TAIL, :].astype(F32)
    number = jnp.broadcast_to(tail[0:1, :] + tail[1:2, :], tail.shape)
    out_ref[k : k + TAIL, :] = halves(number)


def last_kernel(n, *refs):
    before_ref, parts, out_ref = refs[0], refs[1 : 1 + n], refs[1 + n]
    k = before_ref.shape[0]
    centroids, number = updated(before_ref[...].astype(F32), split(parts, 1))
    out_ref[0:k, :] = centroids
    out_ref[k : k + TAIL, :] = jnp.zeros((TAIL, out_ref.shape[1]), F32)
    out_ref[k : k + TAIL, 0:k] = jnp.broadcast_to(number, (TAIL, k))


def output_kernel(bit, mine_ref, theirs_ref, out_ref, number_ref, sems):
    k = out_ref.shape[1]
    core = lax.rem(lax.axis_index("sub"), CORES)
    side = jnp.bitwise_and(jnp.right_shift(lax.axis_index("group"), bit), 1)

    def write(source):
        copy = pltpu.make_async_copy(source.at[0:k], out_ref.at[0], sems.at[0])
        copy.start()
        number_ref[...] = source[k : k + 1, 0:k]
        copy.wait()

    @pl.when(core == side)
    def _():
        write(mine_ref)

    @pl.when(core != side)
    def _():
        write(theirs_ref)


def call(kernel, ins, outs, out_specs=VMEM, scratch=(), flops=0, limit=28 << 20):
    return pl.pallas_call(
        kernel,
        out_shape=outs,
        in_specs=ins,
        out_specs=out_specs,
        scratch_shapes=list(scratch),
        compiler_params=pltpu.CompilerParams(vmem_limit_bytes=limit),
        cost_estimate=pl.CostEstimate(flops=flops, bytes_accessed=1 << 20, transcendentals=0),
    )


class Plan:
    def __init__(self, bit):
        self.mask = 1 << bit
        self.groups = lax.axis_size("group")
        self.subs = lax.axis_size("sub")
        self.chips = self.subs // CORES
        self.bit = bit
        self.far = bit >= FAR

    def devices(self):
        for group in range(self.groups):
            for sub in range(self.subs):
                yield group, sub // CORES, sub % CORES, (group >> self.bit) & 1

    def flat(self, group, chip, core):
        return group * self.subs + chip * CORES + core

    def permute(self, value, target):
        pairs = [(self.flat(*device[:3]), self.flat(*target(*device))) for device in self.devices()]
        return lax.ppermute(value, AXES, pairs)

    def seeds(self, value):
        if self.far:
            step = 1
            while step < self.chips:
                value = value + self.permute(value, lambda group, chip, core, side: (group, chip ^ step, core))
                step *= 2
            return [self.permute(value, self.across), value]
        received = [self.permute(value, self.across)]
        for step in range(1, self.chips):
            received.append(
                self.permute(
                    value,
                    lambda group, chip, core, side: (
                        (group, chip ^ step, core) if core == side else (group ^ self.mask, chip ^ step, 1 - core)
                    ),
                )
            )
        return received

    def across(self, group, chip, core, side):
        return (group ^ self.mask, chip, core) if core == side else (group, chip, 1 - core)

    def sums(self, values):
        if not self.far:
            (value,) = values
            received = [value]
            for flip in (0, 1):
                for step in range(self.chips):
                    if flip or step:
                        received.append(
                            self.permute(
                                value,
                                lambda group, chip, core, side: (group ^ (self.mask * flip), chip ^ step, core),
                            )
                        )
            return received
        moves = [(0, 1 << i) for i in range(self.chips.bit_length() - 1)]
        orders = [moves + [(self.mask, 0)], [(self.mask, 0)] + moves]
        values = list(values)
        for i in range(len(moves) + 1):
            pairs = []
            for value, order in zip(values, orders):
                flip, step = order[i]
                pairs.append(
                    [value, self.permute(value, lambda group, chip, core, side: (group ^ flip, chip ^ step, core))]
                )
            if i < len(moves):
                values = [merge(*pair) for pair in pairs]
        return [part for pair in pairs for part in pair]

    def last_sums(self, value):
        received = [value]
        for step in range(1, self.chips):
            received.append(self.permute(value, lambda group, chip, core, side: (group, chip ^ step, core)))
        for step in range(self.chips):
            received.append(
                self.permute(
                    value,
                    lambda group, chip, core, side: (
                        (group, chip, 1 - core) if core == side else (group ^ self.mask, chip ^ step, core)
                    ),
                )
            )
        return received


def merge(own, other):
    return call(merge_kernel, [VMEM] * 2, jax.ShapeDtypeStruct(own.shape, own.dtype))(own, other)


def swap_cores(value):
    return lax.ppermute(value, "sub", [(sub, sub ^ 1) for sub in range(lax.axis_size("sub"))])


def turned(rows):
    return call(turn_kernel, [VMEM], jax.ShapeDtypeStruct(rows.shape[::-1], rows.dtype))(rows)


def refine(own_marks, other_marks, own_rows, bit, block):
    plan = Plan(bit)
    other_rows = swap_cores(own_rows)
    own_turned, other_turned = turned(own_rows), turned(other_rows)
    k, width = own_marks.shape[0] - TAIL, own_marks.shape[1]
    scale = width / 8.0
    scratch = [pltpu.VMEM((k, width), F32), pltpu.VMEM((TAIL, k), F32)]
    flops = 8 * own_rows.shape[0] * k * width

    def iteration(kernel, inputs, pieces, kept):
        payload = jax.ShapeDtypeStruct((k // pieces + TAIL, width), BF16)
        *parts, centroids = call(
            kernel, [VMEM] * (len(inputs) + 4), [payload] * pieces + [jax.ShapeDtypeStruct((k, width), kept)],
            [VMEM] * (pieces + 1), scratch, flops,
        )(*inputs, own_rows, other_rows, own_turned, other_turned)
        return parts, centroids

    seeds = plan.seeds(own_marks + other_marks)
    pieces = 2 if plan.far else 1
    parts, centroids = iteration(
        partial(first_kernel, bit, block, scale, len(seeds), plan.far), [own_marks, other_marks, *seeds], pieces, BF16
    )
    for left in reversed(range(ITERS - 1)):
        shares = plan.sums(parts)
        parts, centroids = iteration(
            partial(next_kernel, block, scale, len(shares), pieces), [own_marks, other_marks, centroids, *shares],
            pieces if left else 1, F32,
        )
    (parts,) = parts
    shares = plan.last_sums(parts)
    mine = call(
        partial(last_kernel, len(shares)), [VMEM] * (1 + len(shares)), jax.ShapeDtypeStruct((k + TAIL, width), F32)
    )(centroids, *shares)
    return call(
        partial(output_kernel, bit), [VMEM] * 2,
        (jax.ShapeDtypeStruct((1, k, width), F32), jax.ShapeDtypeStruct((1, k), F32)), (HBM, VMEM),
        [pltpu.SemaphoreType.DMA((1,))],
    )(mine, swap_cores(mine))


def local(embeddings, labels, group_bit, init_index):
    k, width = init_index.shape[1], embeddings.shape[1]
    rows = embeddings.shape[0]
    levels = lax.axis_size("group").bit_length() - 1
    own_marks, own_rows = call(
        seed_kernel, [HBM] * 3,
        (jax.ShapeDtypeStruct((k + TAIL, width), BF16), jax.ShapeDtypeStruct((rows, width), BF16)), (VMEM, VMEM),
        [
            pltpu.VMEM((1, k), jnp.int32),
            pltpu.VMEM((1, labels.shape[0]), jnp.int32),
            pltpu.SemaphoreType.DMA((CHUNKS + 2,)),
        ], 2 * k * rows * width, SEED_VMEM,
    )(init_index, labels[None], embeddings)
    other_marks = swap_cores(own_marks)
    block = rows // labels.shape[0]
    return lax.switch(
        group_bit[0],
        [partial(refine, bit=bit, block=block) for bit in range(levels)],
        own_marks, other_marks, own_rows,
    )


def solution(mesh):
    return jax.shard_map(
        local,
        mesh=mesh,
        in_specs=(P(("group", "sub"), None), P(("group", "sub")), P(), P("group", None)),
        out_specs=(P("group", None, None), P("group", None)),
        check_vma=False,
    )
```

```python
from functools import partial

import jax
import jax.numpy as jnp
from jax import lax
from jax.experimental import pallas as pl
from jax.experimental.pallas import tpu as pltpu
from jax.sharding import PartitionSpec as P

ITERS = 2
PRIOR = 1.0
CORES = 2
TAIL = 8
LANES = 128
SEED_VMEM = 60 << 20
CHUNKS = 4
OUT_CHUNKS = 4
BF16, F32 = jnp.bfloat16, jnp.float32
AXES = ("group", "sub")
VMEM = pl.BlockSpec(memory_space=pltpu.VMEM)
HBM = pl.BlockSpec(memory_space=pltpu.HBM)


def contract(a, b, dim_a, dim_b):
    return lax.dot_general(a, b, (((dim_a,), (dim_b,)), ((), ())), preferred_element_type=F32)


def column(row):
    k = row.shape[1]
    diagonal = lax.broadcasted_iota(jnp.int32, (k, k), 0) == lax.broadcasted_iota(jnp.int32, (k, k), 1)
    return jnp.sum(jnp.where(diagonal, row, jnp.zeros_like(row)), axis=1, keepdims=True)


def halves(number):
    high = number.astype(BF16).astype(F32)
    return jnp.where(lax.broadcasted_iota(jnp.int32, number.shape, 0) == 0, high, number - high).astype(BF16)


def tree(terms):
    while len(terms) > 1:
        terms = [terms[i] + terms[i + 1] for i in range(0, len(terms), 2)]
    return terms[0]


def seed_kernel(index_ref, labels_ref, rows_ref, out_ref, held_ref, index, labels, sems):
    chunks = sems.shape[0] - 2
    k, width = index_ref.shape[1], rows_ref.shape[1]
    rows = rows_ref.shape[0]
    size = rows // chunks
    first = pltpu.make_async_copy(index_ref, index, sems.at[chunks])
    first.start()
    second = pltpu.make_async_copy(labels_ref, labels, sems.at[chunks + 1])
    second.start()
    copies = []
    for i in range(chunks):
        span = pl.ds(i * size, size)
        copies.append(pltpu.make_async_copy(rows_ref.at[span], held_ref.at[span], sems.at[i]))
        copies[-1].start()
    first.wait()
    picked = column(index[...].astype(F32)).astype(jnp.int32) - lax.axis_index("sub") * rows
    total = jnp.zeros((k, width), F32)
    for i in range(chunks):
        onehot = (lax.broadcasted_iota(jnp.int32, (k, size), 1) == picked - i * size).astype(F32).astype(BF16)
        copies[i].wait()
        total = total + contract(onehot, held_ref[pl.ds(i * size, size), :], 1, 0)
    out_ref[0:k, :] = total.astype(BF16)
    out_ref[k : k + TAIL, :] = jnp.zeros((TAIL, width), BF16)
    second.wait()
    marks = jnp.concatenate([labels[...].astype(F32), jnp.zeros((1, LANES - labels.shape[1]), F32)], axis=1)
    out_ref[k : k + TAIL, 0:LANES] = jnp.broadcast_to(marks, (TAIL, LANES)).astype(BF16)


def turn_kernel(rows_ref, out_ref):
    out_ref[...] = rows_ref[...].T


def accumulate(half, own, other, out_ref, sums, counts, block, scale):
    core = lax.rem(lax.axis_index("sub"), CORES)
    k, width = half.shape
    square = half.astype(F32)
    norms = jnp.sum(square * square, axis=1, keepdims=True)
    for first, (marks, rows_ref, turned_ref) in ((True, own), (False, other)):
        rows = rows_ref.shape[0]
        kept_marks = (marks[k : k + 1, 0:LANES].astype(F32) == core.astype(F32)).astype(F32)
        logits = (2.0 * contract(half, turned_ref[...], 1, 0) - norms) * (1.0 / scale)
        top = jnp.max(logits, axis=0, keepdims=True)
        e = jnp.exp(logits - top)
        weights = (e * (1.0 / jnp.sum(e, axis=0, keepdims=True))).astype(BF16)
        kept = jnp.concatenate(
            [jnp.broadcast_to(kept_marks[:, j : j + 1], (1, block)) for j in range(rows // block)], axis=1
        ).astype(BF16)
        weights = weights * kept
        part = contract(weights, rows_ref[...], 1, 0)
        number = contract(jnp.ones((TAIL, rows), BF16), weights, 1, 1)
        if first:
            sums[...] = part
            counts[...] = number
        else:
            sums[...] += part
            counts[...] += number
    out_ref[0:k, :] = sums[...].astype(BF16)
    out_ref[k : k + TAIL, :] = jnp.zeros((TAIL, width), BF16)
    out_ref[k : k + TAIL, 0:k] = halves(counts[...])


def owner(bit):
    side = jnp.bitwise_and(jnp.right_shift(lax.axis_index("group"), bit), 1)
    return lax.rem(lax.axis_index("sub"), CORES) == side


def first_kernel(bit, block, scale, n, *refs):
    own_marks, other_marks = refs[:2]
    parts = refs[2 : 2 + n]
    own_rows, other_rows, own_turned, other_turned, out_ref, c_ref, sums, counts = refs[2 + n :]
    k = c_ref.shape[0]
    chip = own_marks[0:k, :].astype(F32) + other_marks[0:k, :].astype(F32)
    centroids = jnp.where(owner(bit), chip, parts[0][0:k, :].astype(F32))
    for part in parts[1:]:
        centroids = centroids + part[0:k, :].astype(F32)
    half = centroids.astype(BF16)
    c_ref[...] = half
    accumulate(
        half, (own_marks, own_rows, own_turned), (other_marks, other_rows, other_turned), out_ref, sums, counts, block,
        scale,
    )


def number_of(tail):
    return tail[0:1, :] + tail[1:2, :]


def next_kernel(block, scale, *refs):
    own_marks, other_marks, before_ref, one, two, own_rows, other_rows, own_turned, other_turned = refs[:9]
    out_ref, c_ref, sums, counts = refs[9:]
    k = c_ref.shape[0]
    tail = one[k : k + TAIL, 0:k].astype(F32) + two[k : k + TAIL, 0:k].astype(F32)
    total = one[0:k, :].astype(F32) + two[0:k, :].astype(F32)
    centroids = (total + PRIOR * before_ref[...].astype(F32)) * (1.0 / (column(number_of(tail)) + PRIOR))
    c_ref[...] = centroids
    accumulate(
        centroids.astype(BF16), (own_marks, own_rows, own_turned), (other_marks, other_rows, other_turned), out_ref,
        sums, counts, block, scale,
    )


def merge_kernel(one, two, out_ref):
    k = one.shape[0] - TAIL
    out_ref[0:k, :] = (one[0:k, :].astype(F32) + two[0:k, :].astype(F32)).astype(BF16)
    tail = one[k : k + TAIL, :].astype(F32) + two[k : k + TAIL, :].astype(F32)
    out_ref[k : k + TAIL, :] = halves(jnp.broadcast_to(number_of(tail), tail.shape))


def share_kernel(bit, before_ref, *refs):
    parts, out_ref = refs[:-1], refs[-1]
    k = before_ref.shape[0]
    mine = owner(bit)
    wide = [part[...].astype(F32) for part in parts]
    if len(parts) == 3:
        chip = lax.axis_index("sub") // CORES
        own, hub_0, hub_1 = wide
        near, far = jnp.where(chip == 0, hub_0, hub_1), jnp.where(chip == 0, hub_1, hub_0)
        total = jnp.where(mine, (own + far) + near, near)
    else:
        total = tree(wide)
        total = jnp.where(mine, total, jnp.zeros_like(total))
    before = PRIOR * before_ref[...]
    out_ref[0:k, :] = total[0:k, :] + jnp.where(mine, before, jnp.zeros_like(before))
    tail = total[k : k + TAIL, :]
    out_ref[k : k + TAIL, :] = jnp.broadcast_to(number_of(tail), tail.shape)


def output_kernel(one, two, out_ref, number_ref, held, sems):
    k = held.shape[0]
    number = one[k : k + 1, 0:k] + two[k : k + 1, 0:k]
    number_ref[...] = number
    factor = 1.0 / (column(number) + PRIOR)
    chunks = sems.shape[0]
    size = k // chunks
    copies = []
    for i in range(chunks):
        span = pl.ds(i * size, size)
        held[span, :] = (one[span, :] + two[span, :]) * factor[i * size : (i + 1) * size]
        copies.append(pltpu.make_async_copy(held.at[span], out_ref.at[0, span], sems.at[i]))
        copies[-1].start()
    for copy in copies:
        copy.wait()


def call(kernel, ins, outs, out_specs=VMEM, scratch=(), flops=0, limit=28 << 20):
    return pl.pallas_call(
        kernel,
        out_shape=outs,
        in_specs=ins,
        out_specs=out_specs,
        scratch_shapes=list(scratch),
        compiler_params=pltpu.CompilerParams(vmem_limit_bytes=limit),
        cost_estimate=pl.CostEstimate(flops=flops, bytes_accessed=1 << 20, transcendentals=0),
    )


class Plan:
    def __init__(self, bit):
        self.mask = 1 << bit
        self.groups = lax.axis_size("group")
        self.subs = lax.axis_size("sub")
        self.chips = self.subs // CORES
        self.bit = bit

    def devices(self):
        for group in range(self.groups):
            for sub in range(self.subs):
                yield group, sub // CORES, sub % CORES, (group >> self.bit) & 1

    def flat(self, group, chip, core):
        return group * self.subs + chip * CORES + core

    def permute(self, value, target):
        pairs = [(self.flat(*device[:3]), self.flat(*target(*device))) for device in self.devices()]
        return lax.ppermute(value, AXES, pairs)

    def seeds(self, value):
        received = [
            self.permute(
                value,
                lambda group, chip, core, side: (
                    (group ^ self.mask, chip, core) if core == side else (group, chip, 1 - core)
                ),
            )
        ]
        for step in range(1, self.chips):
            received.append(
                self.permute(
                    value,
                    lambda group, chip, core, side: (
                        (group, chip ^ step, core) if core == side else (group ^ self.mask, chip ^ step, 1 - core)
                    ),
                )
            )
        return received

    def sums(self, value):
        moves = [(0, 1 << i) for i in range(self.chips.bit_length() - 1)]
        orders = [moves + [(self.mask, 0)], [(self.mask, 0)] + moves]
        for i in range(len(moves) + 1):
            if i:
                value = merge(*pair)

            def target(group, chip, core, side):
                flip, step = orders[core][i]
                return group ^ flip, chip ^ step, core

            pair = value, self.permute(value, target)
        return pair

    def last_sums(self, value):
        received = [value]
        if self.chips == 2:
            for hub in (0, 1):

                def target(group, chip, core, side):
                    if core != side:
                        return group ^ self.mask, hub, core if chip == 0 else 1 - core
                    return group, 1 - hub, core if chip == hub else 1 - core

                received.append(self.permute(value, target))
            return received
        for step in range(1, self.chips):
            received.append(self.permute(value, lambda group, chip, core, side: (group, chip ^ step, core)))
        for step in range(self.chips):
            received.append(
                self.permute(
                    value,
                    lambda group, chip, core, side: (
                        (group, chip, 1 - core) if core == side else (group ^ self.mask, chip ^ step, core)
                    ),
                )
            )
        return received


def merge(own, other):
    return call(merge_kernel, [VMEM] * 2, jax.ShapeDtypeStruct(own.shape, own.dtype))(own, other)


def swap_cores(value):
    return lax.ppermute(value, "sub", [(sub, sub ^ 1) for sub in range(lax.axis_size("sub"))])


def turned(rows):
    return call(turn_kernel, [VMEM], jax.ShapeDtypeStruct(rows.shape[::-1], rows.dtype))(rows)


def refine(own_marks, other_marks, own_rows, bit, block):
    plan = Plan(bit)
    other_rows = swap_cores(own_rows)
    own_turned, other_turned = turned(own_rows), turned(other_rows)
    k, width = own_marks.shape[0] - TAIL, own_marks.shape[1]
    scale = width / 8.0
    scratch = [pltpu.VMEM((k, width), F32), pltpu.VMEM((TAIL, k), F32)]
    flops = 8 * own_rows.shape[0] * k * width

    payload = jax.ShapeDtypeStruct((k + TAIL, width), BF16)

    def iteration(kernel, inputs, kept):
        return call(
            kernel, [VMEM] * (len(inputs) + 4), (payload, jax.ShapeDtypeStruct((k, width), kept)), (VMEM, VMEM),
            scratch, flops,
        )(*inputs, own_rows, other_rows, own_turned, other_turned)

    seeds = plan.seeds(own_marks + other_marks)
    sums, centroids = iteration(
        partial(first_kernel, bit, block, scale, len(seeds)), [own_marks, other_marks, *seeds], BF16
    )
    for _ in range(ITERS - 1):
        sums, centroids = iteration(
            partial(next_kernel, block, scale), [own_marks, other_marks, centroids, *plan.sums(sums)], F32
        )
    parts = plan.last_sums(sums)
    share = call(
        partial(share_kernel, bit), [VMEM] * (1 + len(parts)), jax.ShapeDtypeStruct((k + TAIL, width), F32)
    )(centroids, *parts)
    return call(
        output_kernel, [VMEM] * 2,
        (jax.ShapeDtypeStruct((1, k, width), F32), jax.ShapeDtypeStruct((1, k), F32)), (HBM, VMEM),
        [pltpu.VMEM((k, width), F32), pltpu.SemaphoreType.DMA((OUT_CHUNKS,))],
    )(share, swap_cores(share))


def local(embeddings, labels, group_bit, init_index):
    k, width = init_index.shape[1], embeddings.shape[1]
    rows = embeddings.shape[0]
    levels = lax.axis_size("group").bit_length() - 1
    own_marks, own_rows = call(
        seed_kernel, [HBM] * 3,
        (jax.ShapeDtypeStruct((k + TAIL, width), BF16), jax.ShapeDtypeStruct((rows, width), BF16)), (VMEM, VMEM),
        [
            pltpu.VMEM((1, k), jnp.int32),
            pltpu.VMEM((1, labels.shape[0]), jnp.int32),
            pltpu.SemaphoreType.DMA((CHUNKS + 2,)),
        ], 2 * k * rows * width, SEED_VMEM,
    )(init_index, labels[None], embeddings)
    other_marks = swap_cores(own_marks)
    block = rows // labels.shape[0]
    return lax.switch(
        group_bit[0],
        [partial(refine, bit=bit, block=block) for bit in range(levels)],
        own_marks, other_marks, own_rows,
    )


def solution(mesh):
    return jax.shard_map(
        local,
        mesh=mesh,
        in_specs=(P(("group", "sub"), None), P(("group", "sub")), P(), P("group", None)),
        out_specs=(P("group", None, None), P("group", None)),
        check_vma=False,
    )
```

```python
from functools import partial

import jax
import jax.numpy as jnp
from jax import lax
from jax.experimental import pallas as pl
from jax.experimental.pallas import tpu as pltpu
from jax.sharding import PartitionSpec as P

ITERS = 2
PRIOR = 1.0
CORES = 2
TAIL = 8
LANES = 128
SEED_VMEM = 60 << 20
CHUNKS = 4
OUT_CHUNKS = 4
BF16, F32 = jnp.bfloat16, jnp.float32
AXES = ("group", "sub")
VMEM = pl.BlockSpec(memory_space=pltpu.VMEM)
HBM = pl.BlockSpec(memory_space=pltpu.HBM)


def contract(a, b, dim_a, dim_b):
    return lax.dot_general(a, b, (((dim_a,), (dim_b,)), ((), ())), preferred_element_type=F32)


def column(row):
    k = row.shape[1]
    diagonal = lax.broadcasted_iota(jnp.int32, (k, k), 0) == lax.broadcasted_iota(jnp.int32, (k, k), 1)
    return jnp.sum(jnp.where(diagonal, row, jnp.zeros_like(row)), axis=1, keepdims=True)


def halves(number):
    high = number.astype(BF16).astype(F32)
    return jnp.where(lax.broadcasted_iota(jnp.int32, number.shape, 0) == 0, high, number - high).astype(BF16)


def tree(terms):
    while len(terms) > 1:
        terms = [terms[i] + terms[i + 1] for i in range(0, len(terms), 2)]
    return terms[0]


def seed_kernel(index_ref, labels_ref, rows_ref, out_ref, held_ref, index, labels, sems):
    chunks = sems.shape[0] - 2
    k, width = index_ref.shape[1], rows_ref.shape[1]
    rows = rows_ref.shape[0]
    size = rows // chunks
    first = pltpu.make_async_copy(index_ref, index, sems.at[chunks])
    first.start()
    second = pltpu.make_async_copy(labels_ref, labels, sems.at[chunks + 1])
    second.start()
    copies = []
    for i in range(chunks):
        span = pl.ds(i * size, size)
        copies.append(pltpu.make_async_copy(rows_ref.at[span], held_ref.at[span], sems.at[i]))
        copies[-1].start()
    first.wait()
    picked = column(index[...].astype(F32)).astype(jnp.int32) - lax.axis_index("sub") * rows
    total = jnp.zeros((k, width), F32)
    for i in range(chunks):
        onehot = (lax.broadcasted_iota(jnp.int32, (k, size), 1) == picked - i * size).astype(F32).astype(BF16)
        copies[i].wait()
        total = total + contract(onehot, held_ref[pl.ds(i * size, size), :], 1, 0)
    out_ref[0:k, :] = total.astype(BF16)
    out_ref[k : k + TAIL, :] = jnp.zeros((TAIL, width), BF16)
    second.wait()
    marks = jnp.concatenate([labels[...].astype(F32), jnp.zeros((1, LANES - labels.shape[1]), F32)], axis=1)
    out_ref[k : k + TAIL, 0:LANES] = jnp.broadcast_to(marks, (TAIL, LANES)).astype(BF16)


def hold_kernel(half, rows_ref, *refs):
    held_ref, turned_ref = refs[-2:]
    rows = rows_ref[...]
    held_ref[half] = rows
    turned_ref[half] = rows.T


def accumulate(half, marks, held_ref, turned_ref, out_ref, sums, counts, kept, block, scale):
    core = lax.rem(lax.axis_index("sub"), CORES)
    k, width = half.shape
    rows = held_ref.shape[1]
    square = half.astype(F32)
    norms = jnp.sum(square * square, axis=1, keepdims=True)
    for i, ref in enumerate(marks):
        chosen = (ref[k : k + 1, 0:LANES].astype(F32) == core.astype(F32)).astype(F32)
        wide = jnp.concatenate(
            [jnp.broadcast_to(chosen[:, j : j + 1], (1, block)) for j in range(rows // block)], axis=1
        )
        kept[i] = jnp.broadcast_to(wide, kept.shape[1:])
    sums[...] = jnp.zeros_like(sums)
    counts[...] = jnp.zeros_like(counts)

    @pl.loop(0, CORES)
    def _(i):
        logits = (2.0 * contract(half, turned_ref[i], 1, 0) - norms) * (1.0 / scale)
        top = jnp.max(logits, axis=0, keepdims=True)
        e = jnp.exp(logits - top)
        weights = (e * (1.0 / jnp.sum(e, axis=0, keepdims=True))).astype(BF16)
        weights = weights * kept[i, 0:1, :].astype(BF16)
        sums[...] += contract(weights, held_ref[i], 1, 0)
        counts[...] += contract(jnp.ones((TAIL, rows), BF16), weights, 1, 1)

    out_ref[0:k, :] = sums[...].astype(BF16)
    out_ref[k : k + TAIL, :] = jnp.zeros((TAIL, width), BF16)
    out_ref[k : k + TAIL, 0:k] = halves(counts[...])


def owner(bit):
    side = jnp.bitwise_and(jnp.right_shift(lax.axis_index("group"), bit), 1)
    return lax.rem(lax.axis_index("sub"), CORES) == side


def first_kernel(bit, block, scale, n, *refs):
    own_marks, other_marks = refs[:2]
    parts = refs[2 : 2 + n]
    held, turned, out_ref, c_ref, sums, counts, kept = refs[2 + n :]
    k = c_ref.shape[0]
    chip = own_marks[0:k, :].astype(F32) + other_marks[0:k, :].astype(F32)
    centroids = jnp.where(owner(bit), chip, parts[0][0:k, :].astype(F32))
    for part in parts[1:]:
        centroids = centroids + part[0:k, :].astype(F32)
    half = centroids.astype(BF16)
    c_ref[...] = half
    accumulate(half, (own_marks, other_marks), held, turned, out_ref, sums, counts, kept, block, scale)


def number_of(tail):
    return tail[0:1, :] + tail[1:2, :]


def next_kernel(block, scale, *refs):
    own_marks, other_marks, before_ref, one, two, held, turned, out_ref, c_ref, sums, counts, kept = refs
    k = c_ref.shape[0]
    tail = one[k : k + TAIL, 0:k].astype(F32) + two[k : k + TAIL, 0:k].astype(F32)
    total = one[0:k, :].astype(F32) + two[0:k, :].astype(F32)
    centroids = (total + PRIOR * before_ref[...].astype(F32)) * (1.0 / (column(number_of(tail)) + PRIOR))
    c_ref[...] = centroids
    accumulate(
        centroids.astype(BF16), (own_marks, other_marks), held, turned, out_ref, sums, counts, kept, block, scale
    )


def merge_kernel(one, two, out_ref):
    k = one.shape[0] - TAIL
    out_ref[0:k, :] = (one[0:k, :].astype(F32) + two[0:k, :].astype(F32)).astype(BF16)
    tail = one[k : k + TAIL, :].astype(F32) + two[k : k + TAIL, :].astype(F32)
    out_ref[k : k + TAIL, :] = halves(jnp.broadcast_to(number_of(tail), tail.shape))


def share_kernel(bit, before_ref, *refs):
    parts, out_ref = refs[:-1], refs[-1]
    k = before_ref.shape[0]
    mine = owner(bit)
    wide = [part[...].astype(F32) for part in parts]
    if len(parts) == 3:
        chip = lax.axis_index("sub") // CORES
        own, hub_0, hub_1 = wide
        near, far = jnp.where(chip == 0, hub_0, hub_1), jnp.where(chip == 0, hub_1, hub_0)
        total = jnp.where(mine, (own + far) + near, near)
    else:
        total = tree(wide)
        total = jnp.where(mine, total, jnp.zeros_like(total))
    before = PRIOR * before_ref[...]
    out_ref[0:k, :] = total[0:k, :] + jnp.where(mine, before, jnp.zeros_like(before))
    tail = total[k : k + TAIL, :]
    out_ref[k : k + TAIL, :] = jnp.broadcast_to(number_of(tail), tail.shape)


def output_kernel(one, two, out_ref, number_ref, held, sems):
    k = held.shape[0]
    number = one[k : k + 1, 0:k] + two[k : k + 1, 0:k]
    number_ref[...] = number
    factor = 1.0 / (column(number) + PRIOR)
    chunks = sems.shape[0]
    size = k // chunks
    copies = []
    for i in range(chunks):
        span = pl.ds(i * size, size)
        held[span, :] = (one[span, :] + two[span, :]) * factor[i * size : (i + 1) * size]
        copies.append(pltpu.make_async_copy(held.at[span], out_ref.at[0, span], sems.at[i]))
        copies[-1].start()
    for copy in copies:
        copy.wait()


def call(kernel, ins, outs, out_specs=VMEM, scratch=(), flops=0, limit=28 << 20, aliases=None):
    return pl.pallas_call(
        kernel,
        out_shape=outs,
        in_specs=ins,
        out_specs=out_specs,
        scratch_shapes=list(scratch),
        input_output_aliases=aliases or {},
        compiler_params=pltpu.CompilerParams(vmem_limit_bytes=limit),
        cost_estimate=pl.CostEstimate(flops=flops, bytes_accessed=1 << 20, transcendentals=0),
    )


class Plan:
    def __init__(self, bit):
        self.mask = 1 << bit
        self.groups = lax.axis_size("group")
        self.subs = lax.axis_size("sub")
        self.chips = self.subs // CORES
        self.bit = bit

    def devices(self):
        for group in range(self.groups):
            for sub in range(self.subs):
                yield group, sub // CORES, sub % CORES, (group >> self.bit) & 1

    def flat(self, group, chip, core):
        return group * self.subs + chip * CORES + core

    def permute(self, value, target):
        pairs = [(self.flat(*device[:3]), self.flat(*target(*device))) for device in self.devices()]
        return lax.ppermute(value, AXES, pairs)

    def seeds(self, value):
        received = [
            self.permute(
                value,
                lambda group, chip, core, side: (
                    (group ^ self.mask, chip, core) if core == side else (group, chip, 1 - core)
                ),
            )
        ]
        for step in range(1, self.chips):
            received.append(
                self.permute(
                    value,
                    lambda group, chip, core, side: (
                        (group, chip ^ step, core) if core == side else (group ^ self.mask, chip ^ step, 1 - core)
                    ),
                )
            )
        return received

    def sums(self, value):
        moves = [(0, 1 << i) for i in range(self.chips.bit_length() - 1)]
        orders = [moves + [(self.mask, 0)], [(self.mask, 0)] + moves]
        for i in range(len(moves) + 1):
            if i:
                value = merge(*pair)

            def target(group, chip, core, side):
                flip, step = orders[core][i]
                return group ^ flip, chip ^ step, core

            pair = value, self.permute(value, target)
        return pair

    def last_sums(self, value):
        received = [value]
        if self.chips == 2:
            for hub in (0, 1):

                def target(group, chip, core, side):
                    if core != side:
                        return group ^ self.mask, hub, core if chip == 0 else 1 - core
                    return group, 1 - hub, core if chip == hub else 1 - core

                received.append(self.permute(value, target))
            return received
        for step in range(1, self.chips):
            received.append(self.permute(value, lambda group, chip, core, side: (group, chip ^ step, core)))
        for step in range(self.chips):
            received.append(
                self.permute(
                    value,
                    lambda group, chip, core, side: (
                        (group, chip, 1 - core) if core == side else (group ^ self.mask, chip ^ step, core)
                    ),
                )
            )
        return received


def merge(own, other):
    return call(merge_kernel, [VMEM] * 2, jax.ShapeDtypeStruct(own.shape, own.dtype))(own, other)


def swap_cores(value):
    return lax.ppermute(value, "sub", [(sub, sub ^ 1) for sub in range(lax.axis_size("sub"))])


def refine(own_marks, other_marks, own_rows, bit, block):
    plan = Plan(bit)
    other_rows = swap_cores(own_rows)
    both = [jax.ShapeDtypeStruct((CORES, *shape), BF16) for shape in (own_rows.shape, own_rows.shape[::-1])]
    held = call(partial(hold_kernel, 0), [VMEM], both, [VMEM] * 2)(own_rows)
    held = call(partial(hold_kernel, 1), [VMEM] * 3, both, [VMEM] * 2, aliases={1: 0, 2: 1})(other_rows, *held)
    k, width = own_marks.shape[0] - TAIL, own_marks.shape[1]
    scale = width / 8.0
    scratch = [
        pltpu.VMEM((k, width), F32), pltpu.VMEM((TAIL, k), F32), pltpu.VMEM((CORES, TAIL, own_rows.shape[0]), F32)
    ]
    flops = 8 * own_rows.shape[0] * k * width

    payload = jax.ShapeDtypeStruct((k + TAIL, width), BF16)

    def iteration(kernel, inputs, kept):
        return call(
            kernel, [VMEM] * (len(inputs) + 2), (payload, jax.ShapeDtypeStruct((k, width), kept)), (VMEM, VMEM),
            scratch, flops,
        )(*inputs, *held)

    seeds = plan.seeds((own_marks + other_marks)[0:k])
    sums, centroids = iteration(
        partial(first_kernel, bit, block, scale, len(seeds)), [own_marks, other_marks, *seeds], BF16
    )
    for _ in range(ITERS - 1):
        sums, centroids = iteration(
            partial(next_kernel, block, scale), [own_marks, other_marks, centroids, *plan.sums(sums)], F32
        )
    parts = plan.last_sums(sums)
    share = call(
        partial(share_kernel, bit), [VMEM] * (1 + len(parts)), jax.ShapeDtypeStruct((k + TAIL, width), F32)
    )(centroids, *parts)
    return call(
        output_kernel, [VMEM] * 2,
        (jax.ShapeDtypeStruct((1, k, width), F32), jax.ShapeDtypeStruct((1, k), F32)), (HBM, VMEM),
        [pltpu.VMEM((k, width), F32), pltpu.SemaphoreType.DMA((OUT_CHUNKS,))],
    )(share, swap_cores(share))


def local(embeddings, labels, group_bit, init_index):
    k, width = init_index.shape[1], embeddings.shape[1]
    rows = embeddings.shape[0]
    levels = lax.axis_size("group").bit_length() - 1
    own_marks, own_rows = call(
        seed_kernel, [HBM] * 3,
        (jax.ShapeDtypeStruct((k + TAIL, width), BF16), jax.ShapeDtypeStruct((rows, width), BF16)), (VMEM, VMEM),
        [
            pltpu.VMEM((1, k), jnp.int32),
            pltpu.VMEM((1, labels.shape[0]), jnp.int32),
            pltpu.SemaphoreType.DMA((CHUNKS + 2,)),
        ], 2 * k * rows * width, SEED_VMEM,
    )(init_index, labels[None], embeddings)
    other_marks = swap_cores(own_marks)
    block = rows // labels.shape[0]
    return lax.switch(
        group_bit[0],
        [partial(refine, bit=bit, block=block) for bit in range(levels)],
        own_marks, other_marks, own_rows,
    )


def solution(mesh):
    return jax.shard_map(
        local,
        mesh=mesh,
        in_specs=(P(("group", "sub"), None), P(("group", "sub")), P(), P("group", None)),
        out_specs=(P("group", None, None), P("group", None)),
        check_vma=False,
    )
```

```python
from functools import partial

import jax
import jax.numpy as jnp
from jax import lax
from jax.experimental import pallas as pl
from jax.experimental.pallas import tpu as pltpu
from jax.sharding import PartitionSpec as P

ITERS = 2
PRIOR = 1.0
CORES = 2
TAIL = 8
LANES = 128
SEED_VMEM = 60 << 20
CHUNKS = 4
OUT_CHUNKS = 4
BF16, F32 = jnp.bfloat16, jnp.float32
AXES = ("group", "sub")
VMEM = pl.BlockSpec(memory_space=pltpu.VMEM)
HBM = pl.BlockSpec(memory_space=pltpu.HBM)


def contract(a, b, dim_a, dim_b):
    return lax.dot_general(a, b, (((dim_a,), (dim_b,)), ((), ())), preferred_element_type=F32)


def column(row):
    k = row.shape[1]
    diagonal = lax.broadcasted_iota(jnp.int32, (k, k), 0) == lax.broadcasted_iota(jnp.int32, (k, k), 1)
    return jnp.sum(jnp.where(diagonal, row, jnp.zeros_like(row)), axis=1, keepdims=True)


def halves(number):
    high = number.astype(BF16).astype(F32)
    return jnp.where(lax.broadcasted_iota(jnp.int32, number.shape, 0) == 0, high, number - high).astype(BF16)


def tree(terms):
    while len(terms) > 1:
        terms = [terms[i] + terms[i + 1] for i in range(0, len(terms), 2)]
    return terms[0]


def seed_kernel(index_ref, labels_ref, rows_ref, out_ref, held_ref, index, labels, sems):
    chunks = sems.shape[0] - 2
    k, width = index_ref.shape[1], rows_ref.shape[1]
    rows = rows_ref.shape[0]
    size = rows // chunks
    first = pltpu.make_async_copy(index_ref, index, sems.at[chunks])
    first.start()
    second = pltpu.make_async_copy(labels_ref, labels, sems.at[chunks + 1])
    second.start()
    copies = []
    for i in range(chunks):
        span = pl.ds(i * size, size)
        copies.append(pltpu.make_async_copy(rows_ref.at[span], held_ref.at[span], sems.at[i]))
        copies[-1].start()
    first.wait()
    picked = column(index[...].astype(F32)).astype(jnp.int32) - lax.axis_index("sub") * rows
    total = jnp.zeros((k, width), F32)
    for i in range(chunks):
        onehot = (lax.broadcasted_iota(jnp.int32, (k, size), 1) == picked - i * size).astype(F32).astype(BF16)
        copies[i].wait()
        total = total + contract(onehot, held_ref[pl.ds(i * size, size), :], 1, 0)
    out_ref[0:k, :] = total.astype(BF16)
    out_ref[k : k + TAIL, :] = jnp.zeros((TAIL, width), BF16)
    second.wait()
    marks = jnp.concatenate([labels[...].astype(F32), jnp.zeros((1, LANES - labels.shape[1]), F32)], axis=1)
    out_ref[k : k + TAIL, 0:LANES] = jnp.broadcast_to(marks, (TAIL, LANES)).astype(BF16)


def hold_kernel(half, block, rows_ref, marks_ref, *refs):
    held_ref, turned_ref, kept_ref = refs[-3:]
    rows = rows_ref[...]
    held_ref[half] = rows
    turned_ref[half] = rows.T
    core = lax.rem(lax.axis_index("sub"), CORES)
    k = marks_ref.shape[0] - TAIL
    chosen = (marks_ref[k : k + 1, 0:LANES].astype(F32) == core.astype(F32)).astype(F32)
    wide = [jnp.broadcast_to(chosen[:, j : j + 1], (1, block)) for j in range(rows.shape[0] // block)]
    kept_ref[half] = jnp.broadcast_to(jnp.concatenate(wide, axis=1), kept_ref.shape[1:])


def accumulate(half, held_ref, turned_ref, kept_ref, out_ref, sums, counts, scale):
    k, width = half.shape
    rows = held_ref.shape[1]
    square = half.astype(F32)
    norms = jnp.sum(square * square, axis=1, keepdims=True)

    @pl.loop(0, CORES)
    def _(i):
        logits = (2.0 * contract(half, turned_ref[i], 1, 0) - norms) * (1.0 / scale)
        top = jnp.max(logits, axis=0, keepdims=True)
        e = jnp.exp(logits - top)
        weights = (e * (1.0 / jnp.sum(e, axis=0, keepdims=True))).astype(BF16)
        weights = weights * kept_ref[i, 0:1, :].astype(BF16)
        sums[i] = contract(weights, held_ref[i], 1, 0)
        counts[i] = contract(jnp.ones((TAIL, rows), BF16), weights, 1, 1)

    out_ref[0:k, :] = (sums[0] + sums[1]).astype(BF16)
    out_ref[k : k + TAIL, :] = jnp.zeros((TAIL, width), BF16)
    out_ref[k : k + TAIL, 0:k] = halves(counts[0] + counts[1])


def owner(bit):
    side = jnp.bitwise_and(jnp.right_shift(lax.axis_index("group"), bit), 1)
    return lax.rem(lax.axis_index("sub"), CORES) == side


def first_kernel(bit, scale, n, *refs):
    own_marks, other_marks = refs[:2]
    parts = refs[2 : 2 + n]
    held, turned, kept, out_ref, c_ref, sums, counts = refs[2 + n :]
    k = c_ref.shape[0]
    chip = own_marks[0:k, :].astype(F32) + other_marks[0:k, :].astype(F32)
    centroids = jnp.where(owner(bit), chip, parts[-1][0:k, :].astype(F32))
    for part in parts[:-1]:
        centroids = centroids + part[0:k, :].astype(F32)
    half = centroids.astype(BF16)
    c_ref[...] = half
    accumulate(half, held, turned, kept, out_ref, sums, counts, scale)


def number_of(tail):
    return tail[0:1, :] + tail[1:2, :]


def next_kernel(scale, before_ref, one, two, held, turned, kept, out_ref, c_ref, sums, counts):
    k = c_ref.shape[0]
    tail = one[k : k + TAIL, 0:k].astype(F32) + two[k : k + TAIL, 0:k].astype(F32)
    total = one[0:k, :].astype(F32) + two[0:k, :].astype(F32)
    centroids = (total + PRIOR * before_ref[...].astype(F32)) * (1.0 / (column(number_of(tail)) + PRIOR))
    c_ref[...] = centroids
    accumulate(centroids.astype(BF16), held, turned, kept, out_ref, sums, counts, scale)


def merge_kernel(one, two, out_ref):
    k = one.shape[0] - TAIL
    out_ref[0:k, :] = (one[0:k, :].astype(F32) + two[0:k, :].astype(F32)).astype(BF16)
    tail = one[k : k + TAIL, :].astype(F32) + two[k : k + TAIL, :].astype(F32)
    out_ref[k : k + TAIL, :] = halves(jnp.broadcast_to(number_of(tail), tail.shape))


def share_kernel(bit, before_ref, *refs):
    parts, out_ref = refs[:-1], refs[-1]
    k = before_ref.shape[0]
    mine = owner(bit)
    wide = [part[...].astype(F32) for part in parts]
    if len(parts) == 3:
        chip = lax.axis_index("sub") // CORES
        own, hub_0, hub_1 = wide
        near, far = jnp.where(chip == 0, hub_0, hub_1), jnp.where(chip == 0, hub_1, hub_0)
        total = jnp.where(mine, (own + far) + near, near)
    else:
        total = tree(wide)
        total = jnp.where(mine, total, jnp.zeros_like(total))
    before = PRIOR * before_ref[...]
    out_ref[0:k, :] = total[0:k, :] + jnp.where(mine, before, jnp.zeros_like(before))
    tail = total[k : k + TAIL, :]
    out_ref[k : k + TAIL, :] = jnp.broadcast_to(number_of(tail), tail.shape)


def output_kernel(one, two, out_ref, number_ref, held, sems):
    k = held.shape[0]
    number = one[k : k + 1, 0:k] + two[k : k + 1, 0:k]
    number_ref[...] = number
    factor = 1.0 / (column(number) + PRIOR)
    chunks = sems.shape[0]
    size = k // chunks
    copies = []
    for i in range(chunks):
        span = pl.ds(i * size, size)
        held[span, :] = (one[span, :] + two[span, :]) * factor[i * size : (i + 1) * size]
        copies.append(pltpu.make_async_copy(held.at[span], out_ref.at[0, span], sems.at[i]))
        copies[-1].start()
    for copy in copies:
        copy.wait()


def call(kernel, ins, outs, out_specs=VMEM, scratch=(), flops=0, limit=28 << 20, aliases=None):
    return pl.pallas_call(
        kernel,
        out_shape=outs,
        in_specs=ins,
        out_specs=out_specs,
        scratch_shapes=list(scratch),
        input_output_aliases=aliases or {},
        compiler_params=pltpu.CompilerParams(vmem_limit_bytes=limit),
        cost_estimate=pl.CostEstimate(flops=flops, bytes_accessed=1 << 20, transcendentals=0),
    )


class Plan:
    def __init__(self, bit):
        self.mask = 1 << bit
        self.groups = lax.axis_size("group")
        self.subs = lax.axis_size("sub")
        self.chips = self.subs // CORES
        self.bit = bit

    def devices(self):
        for group in range(self.groups):
            for sub in range(self.subs):
                yield group, sub // CORES, sub % CORES, (group >> self.bit) & 1

    def flat(self, group, chip, core):
        return group * self.subs + chip * CORES + core

    def permute(self, value, target):
        pairs = [(self.flat(*device[:3]), self.flat(*target(*device))) for device in self.devices()]
        return lax.ppermute(value, AXES, pairs)

    def seeds(self, value):
        received = []
        for step in range(1, self.chips):
            received.append(
                self.permute(
                    value,
                    lambda group, chip, core, side: (
                        (group, chip ^ step, core)
                        if core == side
                        else (group ^ self.mask, chip ^ (step - 1), 1 - core)
                    ),
                )
            )
        received.append(
            self.permute(
                value,
                lambda group, chip, core, side: (
                    (group ^ self.mask, chip ^ (self.chips - 1), core) if core == side else (group, chip, 1 - core)
                ),
            )
        )
        return received

    def sums(self, value):
        moves = [(0, 1 << i) for i in range(self.chips.bit_length() - 1)]
        orders = [moves + [(self.mask, 0)], [(self.mask, 0)] + moves]
        for i in range(len(moves) + 1):
            if i:
                value = merge(*pair)

            def target(group, chip, core, side):
                flip, step = orders[core][i]
                return group ^ flip, chip ^ step, core

            pair = value, self.permute(value, target)
        return pair

    def last_sums(self, value):
        received = [value]
        if self.chips == 2:
            for hub in (0, 1):

                def target(group, chip, core, side):
                    if core != side:
                        return group ^ self.mask, hub, core if chip == 0 else 1 - core
                    return group, 1 - hub, core if chip == hub else 1 - core

                received.append(self.permute(value, target))
            return received
        for step in range(1, self.chips):
            received.append(self.permute(value, lambda group, chip, core, side: (group, chip ^ step, core)))
        for step in range(self.chips):
            received.append(
                self.permute(
                    value,
                    lambda group, chip, core, side: (
                        (group, chip, 1 - core) if core == side else (group ^ self.mask, chip ^ step, core)
                    ),
                )
            )
        return received


def merge(own, other):
    return call(merge_kernel, [VMEM] * 2, jax.ShapeDtypeStruct(own.shape, own.dtype))(own, other)


def swap_cores(value):
    return lax.ppermute(value, "sub", [(sub, sub ^ 1) for sub in range(lax.axis_size("sub"))])


def refine(own_marks, other_marks, own_rows, bit, block):
    plan = Plan(bit)
    other_rows = swap_cores(own_rows)
    rows = own_rows.shape[0]
    k, width = own_marks.shape[0] - TAIL, own_marks.shape[1]
    scale = width / 8.0
    scratch = [
        pltpu.VMEM((CORES, k, width), F32), pltpu.VMEM((CORES, TAIL, k), F32)
    ]
    flops = 8 * rows * k * width

    both = [
        jax.ShapeDtypeStruct((CORES, rows, width), BF16),
        jax.ShapeDtypeStruct((CORES, width, rows), BF16),
        jax.ShapeDtypeStruct((CORES, TAIL, rows), F32),
    ]
    held = call(partial(hold_kernel, 0, block), [VMEM] * 2, both, [VMEM] * 3)(own_rows, own_marks)
    held = call(
        partial(hold_kernel, 1, block), [VMEM] * 5, both, [VMEM] * 3, aliases={2: 0, 3: 1, 4: 2}
    )(other_rows, other_marks, *held)
    payload = jax.ShapeDtypeStruct((k + TAIL, width), BF16)

    def iteration(kernel, inputs, kept):
        return call(
            kernel, [VMEM] * (len(inputs) + len(held)), (payload, jax.ShapeDtypeStruct((k, width), kept)), (VMEM, VMEM),
            scratch, flops,
        )(*inputs, *held)

    seeds = plan.seeds((own_marks + other_marks)[0:k])
    sums, centroids = iteration(
        partial(first_kernel, bit, scale, len(seeds)), [own_marks, other_marks, *seeds], BF16
    )
    for _ in range(ITERS - 1):
        sums, centroids = iteration(
            partial(next_kernel, scale), [centroids, *plan.sums(sums)], F32
        )
    parts = plan.last_sums(sums)
    share = call(
        partial(share_kernel, bit), [VMEM] * (1 + len(parts)), jax.ShapeDtypeStruct((k + TAIL, width), F32)
    )(centroids, *parts)
    return call(
        output_kernel, [VMEM] * 2,
        (jax.ShapeDtypeStruct((1, k, width), F32), jax.ShapeDtypeStruct((1, k), F32)), (HBM, VMEM),
        [pltpu.VMEM((k, width), F32), pltpu.SemaphoreType.DMA((OUT_CHUNKS,))],
    )(share, swap_cores(share))


def local(embeddings, labels, group_bit, init_index):
    k, width = init_index.shape[1], embeddings.shape[1]
    rows = embeddings.shape[0]
    levels = lax.axis_size("group").bit_length() - 1
    own_marks, own_rows = call(
        seed_kernel, [HBM] * 3,
        (jax.ShapeDtypeStruct((k + TAIL, width), BF16), jax.ShapeDtypeStruct((rows, width), BF16)), (VMEM, VMEM),
        [
            pltpu.VMEM((1, k), jnp.int32),
            pltpu.VMEM((1, labels.shape[0]), jnp.int32),
            pltpu.SemaphoreType.DMA((CHUNKS + 2,)),
        ], 2 * k * rows * width, SEED_VMEM,
    )(init_index, labels[None], embeddings)
    other_marks = swap_cores(own_marks)
    block = rows // labels.shape[0]
    return lax.switch(
        group_bit[0],
        [partial(refine, bit=bit, block=block) for bit in range(levels)],
        own_marks, other_marks, own_rows,
    )


def solution(mesh):
    return jax.shard_map(
        local,
        mesh=mesh,
        in_specs=(P(("group", "sub"), None), P(("group", "sub")), P(), P("group", None)),
        out_specs=(P("group", None, None), P("group", None)),
        check_vma=False,
    )
```

```python
from functools import partial

import jax
import jax.numpy as jnp
from jax import lax
from jax.experimental import pallas as pl
from jax.experimental.pallas import tpu as pltpu
from jax.sharding import PartitionSpec as P

ITERS = 2
PRIOR = 1.0
CORES = 2
TAIL = 8
LANES = 128
SEED_VMEM = 60 << 20
CHUNKS = 4
OUT_CHUNKS = 4
BF16, F32 = jnp.bfloat16, jnp.float32
AXES = ("group", "sub")
VMEM = pl.BlockSpec(memory_space=pltpu.VMEM)
HBM = pl.BlockSpec(memory_space=pltpu.HBM)


def contract(a, b, dim_a, dim_b):
    return lax.dot_general(a, b, (((dim_a,), (dim_b,)), ((), ())), preferred_element_type=F32)


def column(row):
    k = row.shape[1]
    diagonal = lax.broadcasted_iota(jnp.int32, (k, k), 0) == lax.broadcasted_iota(jnp.int32, (k, k), 1)
    return jnp.sum(jnp.where(diagonal, row, jnp.zeros_like(row)), axis=1, keepdims=True)


def halves(number):
    high = number.astype(BF16).astype(F32)
    return jnp.where(lax.broadcasted_iota(jnp.int32, number.shape, 0) == 0, high, number - high).astype(BF16)


def tree(terms):
    while len(terms) > 1:
        terms = [terms[i] + terms[i + 1] for i in range(0, len(terms), 2)]
    return terms[0]


def seed_kernel(index_ref, labels_ref, rows_ref, out_ref, held_ref, index, labels, sems):
    chunks = sems.shape[0] - 2
    k, width = index_ref.shape[1], rows_ref.shape[1]
    rows = rows_ref.shape[0]
    size = rows // chunks
    first = pltpu.make_async_copy(index_ref, index, sems.at[chunks])
    first.start()
    second = pltpu.make_async_copy(labels_ref, labels, sems.at[chunks + 1])
    second.start()
    copies = []
    for i in range(chunks):
        span = pl.ds(i * size, size)
        copies.append(pltpu.make_async_copy(rows_ref.at[span], held_ref.at[span], sems.at[i]))
        copies[-1].start()
    first.wait()
    picked = column(index[...].astype(F32)).astype(jnp.int32) - lax.axis_index("sub") * rows
    total = jnp.zeros((k, width), F32)
    for i in range(chunks):
        onehot = (lax.broadcasted_iota(jnp.int32, (k, size), 1) == picked - i * size).astype(F32).astype(BF16)
        copies[i].wait()
        total = total + contract(onehot, held_ref[pl.ds(i * size, size), :], 1, 0)
    out_ref[0:k, :] = total.astype(BF16)
    out_ref[k : k + TAIL, :] = jnp.zeros((TAIL, width), BF16)
    second.wait()
    marks = jnp.concatenate([labels[...].astype(F32), jnp.zeros((1, LANES - labels.shape[1]), F32)], axis=1)
    out_ref[k : k + TAIL, 0:LANES] = jnp.broadcast_to(marks, (TAIL, LANES)).astype(BF16)


def hold_kernel(half, block, rows_ref, marks_ref, *refs):
    held_ref, turned_ref, kept_ref = refs[-3:]
    size = rows_ref.shape[0] // 4

    @pl.loop(0, 4)
    def _(i):
        span = pl.ds(pl.multiple_of(i * size, size), size)
        part = rows_ref[span, :]
        held_ref[half, span, :] = part
        turned_ref[half, :, span] = part.T

    core = lax.rem(lax.axis_index("sub"), CORES)
    k = marks_ref.shape[0] - TAIL
    chosen = (marks_ref[k : k + 1, 0:LANES].astype(F32) == core.astype(F32)).astype(F32)
    wide = [jnp.broadcast_to(chosen[:, j : j + 1], (1, block)) for j in range(rows_ref.shape[0] // block)]
    kept_ref[half] = jnp.broadcast_to(jnp.concatenate(wide, axis=1), kept_ref.shape[1:])


def accumulate(half, held_ref, turned_ref, kept_ref, out_ref, sums, counts, scale, unroll):
    k, width = half.shape
    rows = held_ref.shape[1]
    square = half.astype(F32)
    norms = jnp.sum(square * square, axis=1, keepdims=True)

    @pl.loop(0, CORES, unroll=unroll)
    def _(i):
        logits = (2.0 * contract(half, turned_ref[i], 1, 0) - norms) * (1.0 / scale)
        top = jnp.max(logits, axis=0, keepdims=True)
        e = jnp.exp(logits - top)
        weights = (e * (1.0 / jnp.sum(e, axis=0, keepdims=True))).astype(BF16)
        weights = weights * kept_ref[i, 0:1, :].astype(BF16)
        sums[i] = contract(weights, held_ref[i], 1, 0)
        counts[i] = contract(jnp.ones((TAIL, rows), BF16), weights, 1, 1)

    out_ref[0:k, :] = (sums[0] + sums[1]).astype(BF16)
    out_ref[k : k + TAIL, :] = jnp.zeros((TAIL, width), BF16)
    out_ref[k : k + TAIL, 0:k] = halves(counts[0] + counts[1])


def owner(bit):
    side = jnp.bitwise_and(jnp.right_shift(lax.axis_index("group"), bit), 1)
    return lax.rem(lax.axis_index("sub"), CORES) == side


def first_kernel(bit, scale, n, *refs):
    own_marks, other_marks = refs[:2]
    parts = refs[2 : 2 + n]
    held, turned, kept, out_ref, c_ref, sums, counts = refs[2 + n :]
    k = c_ref.shape[0]
    chip = own_marks[0:k, :].astype(F32) + other_marks[0:k, :].astype(F32)
    centroids = jnp.where(owner(bit), chip, parts[-1][0:k, :].astype(F32))
    for part in parts[:-1]:
        centroids = centroids + part[0:k, :].astype(F32)
    half = centroids.astype(BF16)
    c_ref[...] = half
    accumulate(half, held, turned, kept, out_ref, sums, counts, scale, False)


def number_of(tail):
    return tail[0:1, :] + tail[1:2, :]


def next_kernel(scale, before_ref, one, two, held, turned, kept, out_ref, c_ref, sums, counts):
    k = c_ref.shape[0]
    tail = one[k : k + TAIL, 0:k].astype(F32) + two[k : k + TAIL, 0:k].astype(F32)
    total = one[0:k, :].astype(F32) + two[0:k, :].astype(F32)
    centroids = (total + PRIOR * before_ref[...].astype(F32)) * (1.0 / (column(number_of(tail)) + PRIOR))
    c_ref[...] = centroids
    accumulate(centroids.astype(BF16), held, turned, kept, out_ref, sums, counts, scale, True)


def merge_kernel(one, two, out_ref):
    k = one.shape[0] - TAIL
    out_ref[0:k, :] = (one[0:k, :].astype(F32) + two[0:k, :].astype(F32)).astype(BF16)
    tail = one[k : k + TAIL, :].astype(F32) + two[k : k + TAIL, :].astype(F32)
    out_ref[k : k + TAIL, :] = halves(jnp.broadcast_to(number_of(tail), tail.shape))


def share_kernel(bit, before_ref, *refs):
    parts, out_ref = refs[:-1], refs[-1]
    k = before_ref.shape[0]
    mine = owner(bit)
    wide = [part[...].astype(F32) for part in parts]
    if len(parts) == 3:
        chip = lax.axis_index("sub") // CORES
        own, hub_0, hub_1 = wide
        near, far = jnp.where(chip == 0, hub_0, hub_1), jnp.where(chip == 0, hub_1, hub_0)
        total = jnp.where(mine, (own + far) + near, near)
    else:
        total = tree(wide)
        total = jnp.where(mine, total, jnp.zeros_like(total))
    before = PRIOR * before_ref[...]
    out_ref[0:k, :] = total[0:k, :] + jnp.where(mine, before, jnp.zeros_like(before))
    tail = total[k : k + TAIL, :]
    out_ref[k : k + TAIL, :] = jnp.broadcast_to(number_of(tail), tail.shape)


def output_kernel(one, two, out_ref, number_ref, held, row, sems):
    k = held.shape[0]
    number = one[k : k + 1, 0:k] + two[k : k + 1, 0:k]
    row[...] = number
    copies = [pltpu.make_async_copy(row, number_ref, sems.at[OUT_CHUNKS])]
    copies[0].start()
    factor = 1.0 / (column(number) + PRIOR)
    size = k // OUT_CHUNKS
    for i in range(OUT_CHUNKS):
        span = pl.ds(i * size, size)
        held[span, :] = (one[span, :] + two[span, :]) * factor[i * size : (i + 1) * size]
        copies.append(pltpu.make_async_copy(held.at[span], out_ref.at[0, span], sems.at[i]))
        copies[-1].start()
    for copy in copies:
        copy.wait()


def call(kernel, ins, outs, out_specs=VMEM, scratch=(), flops=0, limit=28 << 20, aliases=None):
    return pl.pallas_call(
        kernel,
        out_shape=outs,
        in_specs=ins,
        out_specs=out_specs,
        scratch_shapes=list(scratch),
        input_output_aliases=aliases or {},
        compiler_params=pltpu.CompilerParams(vmem_limit_bytes=limit),
        cost_estimate=pl.CostEstimate(flops=flops, bytes_accessed=1 << 20, transcendentals=0),
    )


class Plan:
    def __init__(self, bit):
        self.mask = 1 << bit
        self.groups = lax.axis_size("group")
        self.subs = lax.axis_size("sub")
        self.chips = self.subs // CORES
        self.bit = bit

    def devices(self):
        for group in range(self.groups):
            for sub in range(self.subs):
                yield group, sub // CORES, sub % CORES, (group >> self.bit) & 1

    def flat(self, group, chip, core):
        return group * self.subs + chip * CORES + core

    def permute(self, value, target):
        pairs = [(self.flat(*device[:3]), self.flat(*target(*device))) for device in self.devices()]
        return lax.ppermute(value, AXES, pairs)

    def seeds(self, value):
        received = []
        for step in range(1, self.chips):
            received.append(
                self.permute(
                    value,
                    lambda group, chip, core, side: (
                        (group, chip ^ step, core)
                        if core == side
                        else (group ^ self.mask, chip ^ (step - 1), 1 - core)
                    ),
                )
            )
        received.append(
            self.permute(
                value,
                lambda group, chip, core, side: (
                    (group ^ self.mask, chip ^ (self.chips - 1), core) if core == side else (group, chip, 1 - core)
                ),
            )
        )
        return received

    def sums(self, value):
        moves = [(0, 1 << i) for i in range(self.chips.bit_length() - 1)]
        orders = [moves + [(self.mask, 0)], [(self.mask, 0)] + moves]
        for i in range(len(moves) + 1):
            if i:
                value = merge(*pair)

            def target(group, chip, core, side):
                flip, step = orders[core][i]
                return group ^ flip, chip ^ step, core

            pair = value, self.permute(value, target)
        return pair

    def last_sums(self, value):
        received = [value]
        if self.chips == 2:
            for hub in (0, 1):

                def target(group, chip, core, side):
                    if core != side:
                        return group ^ self.mask, hub, core if chip == 0 else 1 - core
                    return group, 1 - hub, core if chip == hub else 1 - core

                received.append(self.permute(value, target))
            return received
        for step in range(1, self.chips):
            received.append(self.permute(value, lambda group, chip, core, side: (group, chip ^ step, core)))
        for step in range(self.chips):
            received.append(
                self.permute(
                    value,
                    lambda group, chip, core, side: (
                        (group, chip, 1 - core) if core == side else (group ^ self.mask, chip ^ step, core)
                    ),
                )
            )
        return received


def merge(own, other):
    return call(merge_kernel, [VMEM] * 2, jax.ShapeDtypeStruct(own.shape, own.dtype))(own, other)


def swap_cores(value):
    return lax.ppermute(value, "sub", [(sub, sub ^ 1) for sub in range(lax.axis_size("sub"))])


def refine(own_marks, other_marks, own_rows, bit, block):
    plan = Plan(bit)
    other_rows = swap_cores(own_rows)
    rows = own_rows.shape[0]
    k, width = own_marks.shape[0] - TAIL, own_marks.shape[1]
    scale = width / 8.0
    scratch = [
        pltpu.VMEM((CORES, k, width), F32), pltpu.VMEM((CORES, TAIL, k), F32)
    ]
    flops = 8 * rows * k * width

    both = [
        jax.ShapeDtypeStruct((CORES, rows, width), BF16),
        jax.ShapeDtypeStruct((CORES, width, rows), BF16),
        jax.ShapeDtypeStruct((CORES, TAIL, rows), F32),
    ]
    held = call(partial(hold_kernel, 0, block), [VMEM] * 2, both, [VMEM] * 3)(own_rows, own_marks)
    held = call(
        partial(hold_kernel, 1, block), [VMEM] * 5, both, [VMEM] * 3, aliases={2: 0, 3: 1, 4: 2}
    )(other_rows, other_marks, *held)
    payload = jax.ShapeDtypeStruct((k + TAIL, width), BF16)

    def iteration(kernel, inputs, kept):
        return call(
            kernel, [VMEM] * (len(inputs) + len(held)), (payload, jax.ShapeDtypeStruct((k, width), kept)), (VMEM, VMEM),
            scratch, flops,
        )(*inputs, *held)

    seeds = plan.seeds((own_marks + other_marks)[0:k])
    sums, centroids = iteration(
        partial(first_kernel, bit, scale, len(seeds)), [own_marks, other_marks, *seeds], BF16
    )
    for _ in range(ITERS - 1):
        sums, centroids = iteration(
            partial(next_kernel, scale), [centroids, *plan.sums(sums)], F32
        )
    parts = plan.last_sums(sums)
    return call(
        partial(share_kernel, bit), [VMEM] * (1 + len(parts)), jax.ShapeDtypeStruct((k + TAIL, width), F32)
    )(centroids, *parts)


def local(embeddings, labels, group_bit, init_index):
    k, width = init_index.shape[1], embeddings.shape[1]
    rows = embeddings.shape[0]
    levels = lax.axis_size("group").bit_length() - 1
    own_marks, own_rows = call(
        seed_kernel, [HBM] * 3,
        (jax.ShapeDtypeStruct((k + TAIL, width), BF16), jax.ShapeDtypeStruct((rows, width), BF16)), (VMEM, VMEM),
        [
            pltpu.VMEM((1, k), jnp.int32),
            pltpu.VMEM((1, labels.shape[0]), jnp.int32),
            pltpu.SemaphoreType.DMA((CHUNKS + 2,)),
        ], 2 * k * rows * width, SEED_VMEM,
    )(init_index, labels[None], embeddings)
    other_marks = swap_cores(own_marks)
    block = rows // labels.shape[0]
    share = lax.switch(
        group_bit[0],
        [partial(refine, bit=bit, block=block) for bit in range(levels)],
        own_marks, other_marks, own_rows,
    )
    return call(
        output_kernel, [VMEM] * 2,
        (jax.ShapeDtypeStruct((1, k, width), F32), jax.ShapeDtypeStruct((1, k), F32)), (HBM, HBM),
        [pltpu.VMEM((k, width), F32), pltpu.VMEM((1, k), F32), pltpu.SemaphoreType.DMA((OUT_CHUNKS + 1,))],
    )(share, swap_cores(share))


def solution(mesh):
    return jax.shard_map(
        local,
        mesh=mesh,
        in_specs=(P(("group", "sub"), None), P(("group", "sub")), P(), P("group", None)),
        out_specs=(P("group", None, None), P("group", None)),
        check_vma=False,
    )
```

```python
from functools import partial

import jax
import jax.numpy as jnp
from jax import lax
from jax.experimental import pallas as pl
from jax.experimental.pallas import tpu as pltpu
from jax.sharding import PartitionSpec as P

ITERS = 2
PRIOR = 1.0
CORES = 2
TAIL = 8
LANES = 128
SEED_VMEM = 60 << 20
CHUNKS = 4
OUT_CHUNKS = 4
BF16, F32 = jnp.bfloat16, jnp.float32
AXES = ("group", "sub")
VMEM = pl.BlockSpec(memory_space=pltpu.VMEM)
HBM = pl.BlockSpec(memory_space=pltpu.HBM)


def contract(a, b, dim_a, dim_b):
    return lax.dot_general(a, b, (((dim_a,), (dim_b,)), ((), ())), preferred_element_type=F32)


def column(row):
    k = row.shape[1]
    diagonal = lax.broadcasted_iota(jnp.int32, (k, k), 0) == lax.broadcasted_iota(jnp.int32, (k, k), 1)
    return jnp.sum(jnp.where(diagonal, row, jnp.zeros_like(row)), axis=1, keepdims=True)


def halves(number):
    high = number.astype(BF16).astype(F32)
    return jnp.where(lax.broadcasted_iota(jnp.int32, number.shape, 0) == 0, high, number - high).astype(BF16)


def tree(terms):
    while len(terms) > 1:
        terms = [terms[i] + terms[i + 1] for i in range(0, len(terms), 2)]
    return terms[0]


def seed_kernel(index_ref, labels_ref, rows_ref, out_ref, held_ref, index, labels, total, sems):
    chunks = sems.shape[0] - 2
    k, width = index_ref.shape[1], rows_ref.shape[1]
    rows = rows_ref.shape[0]
    size = rows // chunks
    first = pltpu.make_async_copy(index_ref, index, sems.at[chunks])
    first.start()
    second = pltpu.make_async_copy(labels_ref, labels, sems.at[chunks + 1])
    second.start()
    copies = []
    for i in range(chunks):
        span = pl.ds(i * size, size)
        copies.append(pltpu.make_async_copy(rows_ref.at[span], held_ref.at[span], sems.at[i]))
        copies[-1].start()
    first.wait()
    picked = column(index[...].astype(F32)).astype(jnp.int32) - lax.axis_index("sub") * rows
    total[...] = jnp.zeros_like(total)

    @pl.loop(0, chunks)
    def _(i):
        onehot = (lax.broadcasted_iota(jnp.int32, (k, size), 1) == picked - i * size).astype(F32).astype(BF16)
        span = pl.ds(pl.multiple_of(i * size, size), size)
        pltpu.make_async_copy(rows_ref.at[span], held_ref.at[span], sems.at[i]).wait()
        total[...] += contract(onehot, held_ref[span, :], 1, 0)

    out_ref[0:k, :] = total[...].astype(BF16)
    out_ref[k : k + TAIL, :] = jnp.zeros((TAIL, width), BF16)
    second.wait()
    marks = jnp.concatenate([labels[...].astype(F32), jnp.zeros((1, LANES - labels.shape[1]), F32)], axis=1)
    out_ref[k : k + TAIL, 0:LANES] = jnp.broadcast_to(marks, (TAIL, LANES)).astype(BF16)


def hold_kernel(half, block, rows_ref, marks_ref, *refs):
    held_ref, turned_ref, kept_ref = refs[-3:]
    size = rows_ref.shape[0] // 8

    @pl.loop(0, 8)
    def _(i):
        span = pl.ds(pl.multiple_of(i * size, size), size)
        part = rows_ref[span, :]
        held_ref[half, span, :] = part
        turned_ref[half, :, span] = part.T

    core = lax.rem(lax.axis_index("sub"), CORES)
    k = marks_ref.shape[0] - TAIL
    chosen = (marks_ref[k : k + 1, 0:LANES].astype(F32) == core.astype(F32)).astype(F32)
    wide = [jnp.broadcast_to(chosen[:, j : j + 1], (1, block)) for j in range(rows_ref.shape[0] // block)]
    kept_ref[half] = jnp.broadcast_to(jnp.concatenate(wide, axis=1), kept_ref.shape[1:])


def accumulate(half, held_ref, turned_ref, kept_ref, out_ref, sums, counts, scale, unroll):
    k, width = half.shape
    rows = held_ref.shape[1]
    square = half.astype(F32)
    norms = jnp.sum(square * square, axis=1, keepdims=True)

    @pl.loop(0, CORES, unroll=unroll)
    def _(i):
        logits = (2.0 * contract(half, turned_ref[i], 1, 0) - norms) * (1.0 / scale)
        top = jnp.max(logits, axis=0, keepdims=True)
        e = jnp.exp(logits - top)
        weights = (e * (1.0 / jnp.sum(e, axis=0, keepdims=True))).astype(BF16)
        weights = weights * kept_ref[i, 0:1, :].astype(BF16)
        sums[i] = contract(weights, held_ref[i], 1, 0)
        counts[i] = contract(jnp.ones((TAIL, rows), BF16), weights, 1, 1)

    out_ref[0:k, :] = (sums[0] + sums[1]).astype(BF16)
    out_ref[k : k + TAIL, :] = jnp.zeros((TAIL, width), BF16)
    out_ref[k : k + TAIL, 0:k] = halves(counts[0] + counts[1])


def owner(bit):
    side = jnp.bitwise_and(jnp.right_shift(lax.axis_index("group"), bit), 1)
    return lax.rem(lax.axis_index("sub"), CORES) == side


def first_kernel(bit, scale, n, *refs):
    own_marks, other_marks = refs[:2]
    parts = refs[2 : 2 + n]
    held, turned, kept, out_ref, c_ref, sums, counts = refs[2 + n :]
    k = c_ref.shape[0]
    chip = own_marks[0:k, :].astype(F32) + other_marks[0:k, :].astype(F32)
    centroids = jnp.where(owner(bit), chip, parts[-1][0:k, :].astype(F32))
    for part in parts[:-1]:
        centroids = centroids + part[0:k, :].astype(F32)
    half = centroids.astype(BF16)
    c_ref[...] = half
    accumulate(half, held, turned, kept, out_ref, sums, counts, scale, True)


def number_of(tail):
    return tail[0:1, :] + tail[1:2, :]


def next_kernel(scale, before_ref, one, two, held, turned, kept, out_ref, c_ref, sums, counts):
    k = c_ref.shape[0]
    tail = one[k : k + TAIL, 0:k].astype(F32) + two[k : k + TAIL, 0:k].astype(F32)
    total = one[0:k, :].astype(F32) + two[0:k, :].astype(F32)
    centroids = (total + PRIOR * before_ref[...].astype(F32)) * (1.0 / (column(number_of(tail)) + PRIOR))
    c_ref[...] = centroids
    accumulate(centroids.astype(BF16), held, turned, kept, out_ref, sums, counts, scale, True)


def merge_kernel(one, two, out_ref):
    k = one.shape[0] - TAIL
    out_ref[0:k, :] = (one[0:k, :].astype(F32) + two[0:k, :].astype(F32)).astype(BF16)
    tail = one[k : k + TAIL, :].astype(F32) + two[k : k + TAIL, :].astype(F32)
    out_ref[k : k + TAIL, :] = halves(jnp.broadcast_to(number_of(tail), tail.shape))


def share_kernel(bit, before_ref, *refs):
    parts, out_ref = refs[:-1], refs[-1]
    k = before_ref.shape[0]
    mine = owner(bit)
    wide = [part[...].astype(F32) for part in parts]
    if len(parts) == 3:
        chip = lax.axis_index("sub") // CORES
        own, hub_0, hub_1 = wide
        near, far = jnp.where(chip == 0, hub_0, hub_1), jnp.where(chip == 0, hub_1, hub_0)
        total = jnp.where(mine, (own + far) + near, near)
    else:
        total = tree(wide)
        total = jnp.where(mine, total, jnp.zeros_like(total))
    before = PRIOR * before_ref[...]
    out_ref[0:k, :] = total[0:k, :] + jnp.where(mine, before, jnp.zeros_like(before))
    tail = total[k : k + TAIL, :]
    out_ref[k : k + TAIL, :] = jnp.broadcast_to(number_of(tail), tail.shape)


def output_kernel(one, two, out_ref, number_ref, held, row, sems):
    k = held.shape[0]
    number = one[k : k + 1, 0:k] + two[k : k + 1, 0:k]
    row[...] = number
    copies = [pltpu.make_async_copy(row, number_ref, sems.at[OUT_CHUNKS])]
    copies[0].start()
    factor = 1.0 / (column(number) + PRIOR)
    size = k // OUT_CHUNKS
    for i in range(OUT_CHUNKS):
        span = pl.ds(i * size, size)
        held[span, :] = (one[span, :] + two[span, :]) * factor[i * size : (i + 1) * size]
        copies.append(pltpu.make_async_copy(held.at[span], out_ref.at[0, span], sems.at[i]))
        copies[-1].start()
    for copy in copies:
        copy.wait()


def call(kernel, ins, outs, out_specs=VMEM, scratch=(), flops=0, limit=28 << 20, aliases=None):
    return pl.pallas_call(
        kernel,
        out_shape=outs,
        in_specs=ins,
        out_specs=out_specs,
        scratch_shapes=list(scratch),
        input_output_aliases=aliases or {},
        compiler_params=pltpu.CompilerParams(vmem_limit_bytes=limit),
        cost_estimate=pl.CostEstimate(flops=flops, bytes_accessed=1 << 20, transcendentals=0),
    )


class Plan:
    def __init__(self, bit):
        self.mask = 1 << bit
        self.groups = lax.axis_size("group")
        self.subs = lax.axis_size("sub")
        self.chips = self.subs // CORES
        self.bit = bit

    def devices(self):
        for group in range(self.groups):
            for sub in range(self.subs):
                yield group, sub // CORES, sub % CORES, (group >> self.bit) & 1

    def flat(self, group, chip, core):
        return group * self.subs + chip * CORES + core

    def permute(self, value, target):
        pairs = [(self.flat(*device[:3]), self.flat(*target(*device))) for device in self.devices()]
        return lax.ppermute(value, AXES, pairs)

    def seeds(self, value):
        received = []
        for step in range(1, self.chips):
            received.append(
                self.permute(
                    value,
                    lambda group, chip, core, side: (
                        (group, chip ^ step, core)
                        if core == side
                        else (group ^ self.mask, chip ^ (step - 1), 1 - core)
                    ),
                )
            )
        received.append(
            self.permute(
                value,
                lambda group, chip, core, side: (
                    (group ^ self.mask, chip ^ (self.chips - 1), core) if core == side else (group, chip, 1 - core)
                ),
            )
        )
        return received

    def sums(self, value):
        moves = [(0, 1 << i) for i in range(self.chips.bit_length() - 1)]
        orders = [moves + [(self.mask, 0)], [(self.mask, 0)] + moves]
        for i in range(len(moves) + 1):
            if i:
                value = merge(*pair)

            def target(group, chip, core, side):
                flip, step = orders[core][i]
                return group ^ flip, chip ^ step, core

            pair = value, self.permute(value, target)
        return pair

    def last_sums(self, value):
        received = [value]
        if self.chips == 2:
            for hub in (0, 1):

                def target(group, chip, core, side):
                    if core != side:
                        return group ^ self.mask, hub, core if chip == 0 else 1 - core
                    return group, 1 - hub, core if chip == hub else 1 - core

                received.append(self.permute(value, target))
            return received
        for step in range(1, self.chips):
            received.append(self.permute(value, lambda group, chip, core, side: (group, chip ^ step, core)))
        for step in range(self.chips):
            received.append(
                self.permute(
                    value,
                    lambda group, chip, core, side: (
                        (group, chip, 1 - core) if core == side else (group ^ self.mask, chip ^ step, core)
                    ),
                )
            )
        return received


def merge(own, other):
    return call(merge_kernel, [VMEM] * 2, jax.ShapeDtypeStruct(own.shape, own.dtype))(own, other)


def swap_cores(value):
    return lax.ppermute(value, "sub", [(sub, sub ^ 1) for sub in range(lax.axis_size("sub"))])


def refine(own_marks, other_marks, own_rows, bit, block):
    plan = Plan(bit)
    other_rows = swap_cores(own_rows)
    rows = own_rows.shape[0]
    k, width = own_marks.shape[0] - TAIL, own_marks.shape[1]
    scale = width / 8.0
    scratch = [
        pltpu.VMEM((CORES, k, width), F32), pltpu.VMEM((CORES, TAIL, k), F32)
    ]
    flops = 8 * rows * k * width

    both = [
        jax.ShapeDtypeStruct((CORES, rows, width), BF16),
        jax.ShapeDtypeStruct((CORES, width, rows), BF16),
        jax.ShapeDtypeStruct((CORES, TAIL, rows), F32),
    ]
    held = call(partial(hold_kernel, 0, block), [VMEM] * 2, both, [VMEM] * 3)(own_rows, own_marks)
    held = call(
        partial(hold_kernel, 1, block), [VMEM] * 5, both, [VMEM] * 3, aliases={2: 0, 3: 1, 4: 2}
    )(other_rows, other_marks, *held)
    payload = jax.ShapeDtypeStruct((k + TAIL, width), BF16)

    def iteration(kernel, inputs, kept):
        return call(
            kernel, [VMEM] * (len(inputs) + len(held)), (payload, jax.ShapeDtypeStruct((k, width), kept)), (VMEM, VMEM),
            scratch, flops,
        )(*inputs, *held)

    seeds = plan.seeds((own_marks + other_marks)[0:k])
    sums, centroids = iteration(
        partial(first_kernel, bit, scale, len(seeds)), [own_marks, other_marks, *seeds], BF16
    )
    for _ in range(ITERS - 1):
        sums, centroids = iteration(
            partial(next_kernel, scale), [centroids, *plan.sums(sums)], F32
        )
    parts = plan.last_sums(sums)
    share = call(
        partial(share_kernel, bit), [VMEM] * (1 + len(parts)), jax.ShapeDtypeStruct((k + TAIL, width), F32)
    )(centroids, *parts)
    return call(
        output_kernel, [VMEM] * 2,
        (jax.ShapeDtypeStruct((1, k, width), F32), jax.ShapeDtypeStruct((1, k), F32)), (HBM, HBM),
        [pltpu.VMEM((k, width), F32), pltpu.VMEM((1, k), F32), pltpu.SemaphoreType.DMA((OUT_CHUNKS + 1,))],
    )(share, swap_cores(share))


def local(embeddings, labels, group_bit, init_index):
    k, width = init_index.shape[1], embeddings.shape[1]
    rows = embeddings.shape[0]
    levels = lax.axis_size("group").bit_length() - 1
    own_marks, own_rows = call(
        seed_kernel, [HBM] * 3,
        (jax.ShapeDtypeStruct((k + TAIL, width), BF16), jax.ShapeDtypeStruct((rows, width), BF16)), (VMEM, VMEM),
        [
            pltpu.VMEM((1, k), jnp.int32),
            pltpu.VMEM((1, labels.shape[0]), jnp.int32),
            pltpu.VMEM((k, width), F32),
            pltpu.SemaphoreType.DMA((CHUNKS + 2,)),
        ], 2 * k * rows * width, SEED_VMEM,
    )(init_index, labels[None], embeddings)
    other_marks = swap_cores(own_marks)
    block = rows // labels.shape[0]
    return lax.switch(
        group_bit[0],
        [partial(refine, bit=bit, block=block) for bit in range(levels)],
        own_marks, other_marks, own_rows,
    )


def solution(mesh):
    return jax.shard_map(
        local,
        mesh=mesh,
        in_specs=(P(("group", "sub"), None), P(("group", "sub")), P(), P("group", None)),
        out_specs=(P("group", None, None), P("group", None)),
        check_vma=False,
    )
```

```python
from functools import partial

import jax
import jax.numpy as jnp
from jax import lax
from jax.experimental import pallas as pl
from jax.experimental.pallas import tpu as pltpu
from jax.sharding import PartitionSpec as P

ITERS = 2
PRIOR = 1.0
CORES = 2
TAIL = 8
LANES = 128
FAR = 2
SEED_VMEM = 60 << 20
CHUNKS = 4
OUT_CHUNKS = 4
BF16, F32 = jnp.bfloat16, jnp.float32
AXES = ("group", "sub")
VMEM = pl.BlockSpec(memory_space=pltpu.VMEM)
HBM = pl.BlockSpec(memory_space=pltpu.HBM)


def contract(a, b, dim_a, dim_b):
    return lax.dot_general(a, b, (((dim_a,), (dim_b,)), ((), ())), preferred_element_type=F32)


def column(row):
    k = row.shape[1]
    diagonal = lax.broadcasted_iota(jnp.int32, (k, k), 0) == lax.broadcasted_iota(jnp.int32, (k, k), 1)
    return jnp.sum(jnp.where(diagonal, row, jnp.zeros_like(row)), axis=1, keepdims=True)


def halves(number):
    high = number.astype(BF16).astype(F32)
    return jnp.where(lax.broadcasted_iota(jnp.int32, number.shape, 0) == 0, high, number - high).astype(BF16)


def tree(terms):
    while len(terms) > 1:
        terms = [terms[i] + terms[i + 1] for i in range(0, len(terms), 2)]
    return terms[0]


def seed_kernel(index_ref, labels_ref, rows_ref, out_ref, held_ref, index, labels, total, sems):
    chunks = sems.shape[0] - 2
    k, width = index_ref.shape[1], rows_ref.shape[1]
    rows = rows_ref.shape[0]
    size = rows // chunks
    first = pltpu.make_async_copy(index_ref, index, sems.at[chunks])
    first.start()
    second = pltpu.make_async_copy(labels_ref, labels, sems.at[chunks + 1])
    second.start()
    copies = []
    for i in range(chunks):
        span = pl.ds(i * size, size)
        copies.append(pltpu.make_async_copy(rows_ref.at[span], held_ref.at[span], sems.at[i]))
        copies[-1].start()
    first.wait()
    picked = column(index[...].astype(F32)).astype(jnp.int32) - lax.axis_index("sub") * rows
    total[...] = jnp.zeros_like(total)

    @pl.loop(0, chunks)
    def _(i):
        onehot = (lax.broadcasted_iota(jnp.int32, (k, size), 1) == picked - i * size).astype(F32).astype(BF16)
        span = pl.ds(pl.multiple_of(i * size, size), size)
        pltpu.make_async_copy(rows_ref.at[span], held_ref.at[span], sems.at[i]).wait()
        total[...] += contract(onehot, held_ref[span, :], 1, 0)

    out_ref[0:k, :] = total[...].astype(BF16)
    out_ref[k : k + TAIL, :] = jnp.zeros((TAIL, width), BF16)
    second.wait()
    marks = jnp.concatenate([labels[...].astype(F32), jnp.zeros((1, LANES - labels.shape[1]), F32)], axis=1)
    out_ref[k : k + TAIL, 0:LANES] = jnp.broadcast_to(marks, (TAIL, LANES)).astype(BF16)


def hold_kernel(half, block, rows_ref, marks_ref, *refs):
    held_ref, turned_ref, kept_ref = refs[-3:]
    size = rows_ref.shape[0] // 8

    @pl.loop(0, 8)
    def _(i):
        span = pl.ds(pl.multiple_of(i * size, size), size)
        part = rows_ref[span, :]
        held_ref[half, span, :] = part
        turned_ref[half, :, span] = part.T

    core = lax.rem(lax.axis_index("sub"), CORES)
    k = marks_ref.shape[0] - TAIL
    chosen = (marks_ref[k : k + 1, 0:LANES].astype(F32) == core.astype(F32)).astype(F32)
    wide = [jnp.broadcast_to(chosen[:, j : j + 1], (1, block)) for j in range(rows_ref.shape[0] // block)]
    kept_ref[half] = jnp.broadcast_to(jnp.concatenate(wide, axis=1), kept_ref.shape[1:])


def accumulate(half, held_ref, turned_ref, kept_ref, out_ref, sums, counts, scale, unroll):
    k, width = half.shape
    rows = held_ref.shape[1]
    square = half.astype(F32)
    norms = jnp.sum(square * square, axis=1, keepdims=True)

    @pl.loop(0, CORES, unroll=unroll)
    def _(i):
        logits = (2.0 * contract(half, turned_ref[i], 1, 0) - norms) * (1.0 / scale)
        top = jnp.max(logits, axis=0, keepdims=True)
        e = jnp.exp(logits - top)
        weights = (e * (1.0 / jnp.sum(e, axis=0, keepdims=True))).astype(BF16)
        weights = weights * kept_ref[i, 0:1, :].astype(BF16)
        sums[i] = contract(weights, held_ref[i], 1, 0)
        counts[i] = contract(jnp.ones((TAIL, rows), BF16), weights, 1, 1)

    out_ref[0:k, :] = (sums[0] + sums[1]).astype(BF16)
    out_ref[k : k + TAIL, :] = jnp.zeros((TAIL, width), BF16)
    out_ref[k : k + TAIL, 0:k] = halves(counts[0] + counts[1])


def owner(bit):
    side = jnp.bitwise_and(jnp.right_shift(lax.axis_index("group"), bit), 1)
    return lax.rem(lax.axis_index("sub"), CORES) == side


def first_kernel(bit, scale, n, *refs):
    own_marks, other_marks = refs[:2]
    parts = refs[2 : 2 + n]
    held, turned, kept, out_ref, c_ref, sums, counts = refs[2 + n :]
    k = c_ref.shape[0]
    chip = own_marks[0:k, :].astype(F32) + other_marks[0:k, :].astype(F32)
    centroids = jnp.where(owner(bit), chip, parts[-1][0:k, :].astype(F32))
    for part in parts[:-1]:
        centroids = centroids + part[0:k, :].astype(F32)
    half = centroids.astype(BF16)
    c_ref[...] = half
    accumulate(half, held, turned, kept, out_ref, sums, counts, scale, True)


def number_of(tail):
    return tail[0:1, :] + tail[1:2, :]


def next_kernel(scale, before_ref, one, two, held, turned, kept, out_ref, c_ref, sums, counts):
    k = c_ref.shape[0]
    tail = one[k : k + TAIL, 0:k].astype(F32) + two[k : k + TAIL, 0:k].astype(F32)
    total = one[0:k, :].astype(F32) + two[0:k, :].astype(F32)
    centroids = (total + PRIOR * before_ref[...].astype(F32)) * (1.0 / (column(number_of(tail)) + PRIOR))
    c_ref[...] = centroids
    accumulate(centroids.astype(BF16), held, turned, kept, out_ref, sums, counts, scale, True)


def merge_kernel(one, two, out_ref):
    k = one.shape[0] - TAIL
    out_ref[0:k, :] = (one[0:k, :].astype(F32) + two[0:k, :].astype(F32)).astype(BF16)
    tail = one[k : k + TAIL, :].astype(F32) + two[k : k + TAIL, :].astype(F32)
    out_ref[k : k + TAIL, :] = halves(jnp.broadcast_to(number_of(tail), tail.shape))


def share_kernel(bit, before_ref, *refs):
    parts, out_ref = refs[:-1], refs[-1]
    k = before_ref.shape[0]
    mine = owner(bit)
    wide = [part[...].astype(F32) for part in parts]
    if len(parts) == 3:
        chip = lax.axis_index("sub") // CORES
        own, hub_0, hub_1 = wide
        near, far = jnp.where(chip == 0, hub_0, hub_1), jnp.where(chip == 0, hub_1, hub_0)
        total = jnp.where(mine, (own + far) + near, near)
    else:
        total = tree(wide)
        total = jnp.where(mine, total, jnp.zeros_like(total))
    before = PRIOR * before_ref[...]
    out_ref[0:k, :] = total[0:k, :] + jnp.where(mine, before, jnp.zeros_like(before))
    tail = total[k : k + TAIL, :]
    out_ref[k : k + TAIL, :] = jnp.broadcast_to(number_of(tail), tail.shape)


def output_kernel(one, two, out_ref, number_ref, held, row, sems):
    k = held.shape[0]
    number = one[k : k + 1, 0:k] + two[k : k + 1, 0:k]
    row[...] = number
    copies = [pltpu.make_async_copy(row, number_ref, sems.at[OUT_CHUNKS])]
    copies[0].start()
    factor = 1.0 / (column(number) + PRIOR)
    size = k // OUT_CHUNKS
    for i in range(OUT_CHUNKS):
        span = pl.ds(i * size, size)
        held[span, :] = (one[span, :] + two[span, :]) * factor[i * size : (i + 1) * size]
        copies.append(pltpu.make_async_copy(held.at[span], out_ref.at[0, span], sems.at[i]))
        copies[-1].start()
    for copy in copies:
        copy.wait()


def call(kernel, ins, outs, out_specs=VMEM, scratch=(), flops=0, limit=28 << 20, aliases=None):
    return pl.pallas_call(
        kernel,
        out_shape=outs,
        in_specs=ins,
        out_specs=out_specs,
        scratch_shapes=list(scratch),
        input_output_aliases=aliases or {},
        compiler_params=pltpu.CompilerParams(vmem_limit_bytes=limit),
        cost_estimate=pl.CostEstimate(flops=flops, bytes_accessed=1 << 20, transcendentals=0),
    )


class Plan:
    def __init__(self, bit):
        self.mask = 1 << bit
        self.groups = lax.axis_size("group")
        self.subs = lax.axis_size("sub")
        self.chips = self.subs // CORES
        self.bit = bit

    def devices(self):
        for group in range(self.groups):
            for sub in range(self.subs):
                yield group, sub // CORES, sub % CORES, (group >> self.bit) & 1

    def flat(self, group, chip, core):
        return group * self.subs + chip * CORES + core

    def permute(self, value, target):
        pairs = [(self.flat(*device[:3]), self.flat(*target(*device))) for device in self.devices()]
        return lax.ppermute(value, AXES, pairs)

    def seeds(self, value):
        received = []
        for step in range(1, self.chips):
            received.append(
                self.permute(
                    value,
                    lambda group, chip, core, side: (
                        (group, chip ^ step, core)
                        if core == side
                        else (group ^ self.mask, chip ^ (step - 1), 1 - core)
                    ),
                )
            )
        if self.bit >= FAR and self.chips == 2:
            received.append(self.permute(received[0], lambda group, chip, core, side: (group, 1 - chip, core)))
            return received
        received.append(
            self.permute(
                value,
                lambda group, chip, core, side: (
                    (group ^ self.mask, chip ^ (self.chips - 1), core) if core == side else (group, chip, 1 - core)
                ),
            )
        )
        return received

    def sums(self, value):
        moves = [(0, 1 << i) for i in range(self.chips.bit_length() - 1)]
        orders = [moves + [(self.mask, 0)], [(self.mask, 0)] + moves]
        for i in range(len(moves) + 1):
            if i:
                value = merge(*pair)

            def target(group, chip, core, side):
                flip, step = orders[core][i]
                return group ^ flip, chip ^ step, core

            pair = value, self.permute(value, target)
        return pair

    def last_sums(self, value):
        received = [value]
        if self.chips == 2:
            for hub in (0, 1):

                def target(group, chip, core, side):
                    if core != side:
                        return group ^ self.mask, hub, core if chip == 0 else 1 - core
                    return group, 1 - hub, core if chip == hub else 1 - core

                received.append(self.permute(value, target))
            return received
        for step in range(1, self.chips):
            received.append(self.permute(value, lambda group, chip, core, side: (group, chip ^ step, core)))
        for step in range(self.chips):
            received.append(
                self.permute(
                    value,
                    lambda group, chip, core, side: (
                        (group, chip, 1 - core) if core == side else (group ^ self.mask, chip ^ step, core)
                    ),
                )
            )
        return received


def merge(own, other):
    return call(merge_kernel, [VMEM] * 2, jax.ShapeDtypeStruct(own.shape, own.dtype))(own, other)


def swap_cores(value):
    return lax.ppermute(value, "sub", [(sub, sub ^ 1) for sub in range(lax.axis_size("sub"))])


def refine(own_marks, other_marks, own_rows, bit, block):
    plan = Plan(bit)
    other_rows = swap_cores(own_rows)
    rows = own_rows.shape[0]
    k, width = own_marks.shape[0] - TAIL, own_marks.shape[1]
    scale = width / 8.0
    scratch = [
        pltpu.VMEM((CORES, k, width), F32), pltpu.VMEM((CORES, TAIL, k), F32)
    ]
    flops = 8 * rows * k * width

    both = [
        jax.ShapeDtypeStruct((CORES, rows, width), BF16),
        jax.ShapeDtypeStruct((CORES, width, rows), BF16),
        jax.ShapeDtypeStruct((CORES, TAIL, rows), F32),
    ]
    held = call(partial(hold_kernel, 0, block), [VMEM] * 2, both, [VMEM] * 3)(own_rows, own_marks)
    held = call(
        partial(hold_kernel, 1, block), [VMEM] * 5, both, [VMEM] * 3, aliases={2: 0, 3: 1, 4: 2}
    )(other_rows, other_marks, *held)
    payload = jax.ShapeDtypeStruct((k + TAIL, width), BF16)

    def iteration(kernel, inputs, kept):
        return call(
            kernel, [VMEM] * (len(inputs) + len(held)), (payload, jax.ShapeDtypeStruct((k, width), kept)), (VMEM, VMEM),
            scratch, flops,
        )(*inputs, *held)

    seeds = plan.seeds((own_marks + other_marks)[0:k])
    sums, centroids = iteration(
        partial(first_kernel, bit, scale, len(seeds)), [own_marks, other_marks, *seeds], BF16
    )
    for _ in range(ITERS - 1):
        sums, centroids = iteration(
            partial(next_kernel, scale), [centroids, *plan.sums(sums)], F32
        )
    parts = plan.last_sums(sums)
    share = call(
        partial(share_kernel, bit), [VMEM] * (1 + len(parts)), jax.ShapeDtypeStruct((k + TAIL, width), F32)
    )(centroids, *parts)
    return call(
        output_kernel, [VMEM] * 2,
        (jax.ShapeDtypeStruct((1, k, width), F32), jax.ShapeDtypeStruct((1, k), F32)), (HBM, HBM),
        [pltpu.VMEM((k, width), F32), pltpu.VMEM((1, k), F32), pltpu.SemaphoreType.DMA((OUT_CHUNKS + 1,))],
    )(share, swap_cores(share))


def local(embeddings, labels, group_bit, init_index):
    k, width = init_index.shape[1], embeddings.shape[1]
    rows = embeddings.shape[0]
    levels = lax.axis_size("group").bit_length() - 1
    own_marks, own_rows = call(
        seed_kernel, [HBM] * 3,
        (jax.ShapeDtypeStruct((k + TAIL, width), BF16), jax.ShapeDtypeStruct((rows, width), BF16)), (VMEM, VMEM),
        [
            pltpu.VMEM((1, k), jnp.int32),
            pltpu.VMEM((1, labels.shape[0]), jnp.int32),
            pltpu.VMEM((k, width), F32),
            pltpu.SemaphoreType.DMA((CHUNKS + 2,)),
        ], 2 * k * rows * width, SEED_VMEM,
    )(init_index, labels[None], embeddings)
    other_marks = swap_cores(own_marks)
    block = rows // labels.shape[0]
    return lax.switch(
        group_bit[0],
        [partial(refine, bit=bit, block=block) for bit in range(levels)],
        own_marks, other_marks, own_rows,
    )


def solution(mesh):
    return jax.shard_map(
        local,
        mesh=mesh,
        in_specs=(P(("group", "sub"), None), P(("group", "sub")), P(), P("group", None)),
        out_specs=(P("group", None, None), P("group", None)),
        check_vma=False,
    )
```

```python
from functools import partial

import jax
import jax.numpy as jnp
from jax import lax
from jax.experimental import pallas as pl
from jax.experimental.pallas import tpu as pltpu
from jax.sharding import PartitionSpec as P

ITERS = 2
PRIOR = 1.0
CORES = 2
TAIL = 8
LANES = 128
FAR = 2
SEED_VMEM = 60 << 20
CHUNKS = 2
OUT_CHUNKS = 4
BF16, F32 = jnp.bfloat16, jnp.float32
AXES = ("group", "sub")
VMEM = pl.BlockSpec(memory_space=pltpu.VMEM)
HBM = pl.BlockSpec(memory_space=pltpu.HBM)


def contract(a, b, dim_a, dim_b):
    return lax.dot_general(a, b, (((dim_a,), (dim_b,)), ((), ())), preferred_element_type=F32)


def column(row):
    k = row.shape[1]
    diagonal = lax.broadcasted_iota(jnp.int32, (k, k), 0) == lax.broadcasted_iota(jnp.int32, (k, k), 1)
    return jnp.sum(jnp.where(diagonal, row, jnp.zeros_like(row)), axis=1, keepdims=True)


def halves(number):
    high = number.astype(BF16).astype(F32)
    return jnp.where(lax.broadcasted_iota(jnp.int32, number.shape, 0) == 0, high, number - high).astype(BF16)


def tree(terms):
    while len(terms) > 1:
        terms = [terms[i] + terms[i + 1] for i in range(0, len(terms), 2)]
    return terms[0]


def seed_kernel(index_ref, labels_ref, rows_ref, out_ref, held_ref, index, labels, total, sems):
    chunks = sems.shape[0] - 2
    k, width = index_ref.shape[1], rows_ref.shape[1]
    rows = rows_ref.shape[0]
    size = rows // chunks
    first = pltpu.make_async_copy(index_ref, index, sems.at[chunks])
    first.start()
    second = pltpu.make_async_copy(labels_ref, labels, sems.at[chunks + 1])
    second.start()
    copies = []
    for i in range(chunks):
        span = pl.ds(i * size, size)
        copies.append(pltpu.make_async_copy(rows_ref.at[span], held_ref.at[span], sems.at[i]))
        copies[-1].start()
    first.wait()
    picked = column(index[...].astype(F32)).astype(jnp.int32) - lax.axis_index("sub") * rows
    total[...] = jnp.zeros_like(total)

    @pl.loop(0, chunks)
    def _(i):
        onehot = (lax.broadcasted_iota(jnp.int32, (k, size), 1) == picked - i * size).astype(F32).astype(BF16)
        span = pl.ds(pl.multiple_of(i * size, size), size)
        pltpu.make_async_copy(rows_ref.at[span], held_ref.at[span], sems.at[i]).wait()
        total[...] += contract(onehot, held_ref[span, :], 1, 0)

    out_ref[0:k, :] = total[...].astype(BF16)
    out_ref[k : k + TAIL, :] = jnp.zeros((TAIL, width), BF16)
    second.wait()
    marks = jnp.concatenate([labels[...].astype(F32), jnp.zeros((1, LANES - labels.shape[1]), F32)], axis=1)
    out_ref[k : k + TAIL, 0:LANES] = jnp.broadcast_to(marks, (TAIL, LANES)).astype(BF16)


def hold_kernel(half, block, rows_ref, marks_ref, *refs):
    held_ref, turned_ref, kept_ref = refs[-3:]
    size = rows_ref.shape[0] // 8

    @pl.loop(0, 8)
    def _(i):
        span = pl.ds(pl.multiple_of(i * size, size), size)
        part = rows_ref[span, :]
        held_ref[half, span, :] = part
        turned_ref[half, :, span] = part.T

    core = lax.rem(lax.axis_index("sub"), CORES)
    k = marks_ref.shape[0] - TAIL
    chosen = (marks_ref[k : k + 1, 0:LANES].astype(F32) == core.astype(F32)).astype(F32)
    wide = [jnp.broadcast_to(chosen[:, j : j + 1], (1, block)) for j in range(rows_ref.shape[0] // block)]
    kept_ref[half] = jnp.broadcast_to(jnp.concatenate(wide, axis=1), kept_ref.shape[1:])


def accumulate(half, held_ref, turned_ref, kept_ref, out_ref, sums, counts, scale, unroll):
    k, width = half.shape
    rows = held_ref.shape[1]
    square = half.astype(F32)
    norms = jnp.sum(square * square, axis=1, keepdims=True)

    @pl.loop(0, CORES, unroll=unroll)
    def _(i):
        logits = (2.0 * contract(half, turned_ref[i], 1, 0) - norms) * (1.0 / scale)
        top = jnp.max(logits, axis=0, keepdims=True)
        e = jnp.exp(logits - top)
        weights = (e * (1.0 / jnp.sum(e, axis=0, keepdims=True))).astype(BF16)
        weights = weights * kept_ref[i, 0:1, :].astype(BF16)
        sums[i] = contract(weights, held_ref[i], 1, 0)
        counts[i] = contract(jnp.ones((TAIL, rows), BF16), weights, 1, 1)

    out_ref[0:k, :] = (sums[0] + sums[1]).astype(BF16)
    out_ref[k : k + TAIL, :] = jnp.zeros((TAIL, width), BF16)
    out_ref[k : k + TAIL, 0:k] = halves(counts[0] + counts[1])


def owner(bit):
    side = jnp.bitwise_and(jnp.right_shift(lax.axis_index("group"), bit), 1)
    return lax.rem(lax.axis_index("sub"), CORES) == side


def first_kernel(bit, scale, n, *refs):
    own_marks, other_marks = refs[:2]
    parts = refs[2 : 2 + n]
    held, turned, kept, out_ref, c_ref, sums, counts = refs[2 + n :]
    k = c_ref.shape[0]
    chip = own_marks[0:k, :].astype(F32) + other_marks[0:k, :].astype(F32)
    centroids = jnp.where(owner(bit), chip, parts[-1][0:k, :].astype(F32))
    for part in parts[:-1]:
        centroids = centroids + part[0:k, :].astype(F32)
    half = centroids.astype(BF16)
    c_ref[...] = half
    accumulate(half, held, turned, kept, out_ref, sums, counts, scale, True)


def number_of(tail):
    return tail[0:1, :] + tail[1:2, :]


def next_kernel(scale, before_ref, one, two, held, turned, kept, out_ref, c_ref, sums, counts):
    k = c_ref.shape[0]
    tail = one[k : k + TAIL, 0:k].astype(F32) + two[k : k + TAIL, 0:k].astype(F32)
    total = one[0:k, :].astype(F32) + two[0:k, :].astype(F32)
    centroids = (total + PRIOR * before_ref[...].astype(F32)) * (1.0 / (column(number_of(tail)) + PRIOR))
    c_ref[...] = centroids
    accumulate(centroids.astype(BF16), held, turned, kept, out_ref, sums, counts, scale, True)


def merge_kernel(one, two, out_ref):
    k = one.shape[0] - TAIL
    out_ref[0:k, :] = (one[0:k, :].astype(F32) + two[0:k, :].astype(F32)).astype(BF16)
    tail = one[k : k + TAIL, :].astype(F32) + two[k : k + TAIL, :].astype(F32)
    out_ref[k : k + TAIL, :] = halves(jnp.broadcast_to(number_of(tail), tail.shape))


def share_kernel(bit, before_ref, *refs):
    parts, out_ref = refs[:-1], refs[-1]
    k = before_ref.shape[0]
    mine = owner(bit)
    wide = [part[...].astype(F32) for part in parts]
    if len(parts) == 3:
        chip = lax.axis_index("sub") // CORES
        own, hub_0, hub_1 = wide
        near, far = jnp.where(chip == 0, hub_0, hub_1), jnp.where(chip == 0, hub_1, hub_0)
        total = jnp.where(mine, (own + far) + near, near)
    else:
        total = tree(wide)
        total = jnp.where(mine, total, jnp.zeros_like(total))
    before = PRIOR * before_ref[...]
    out_ref[0:k, :] = total[0:k, :] + jnp.where(mine, before, jnp.zeros_like(before))
    tail = total[k : k + TAIL, :]
    out_ref[k : k + TAIL, :] = jnp.broadcast_to(number_of(tail), tail.shape)


def output_kernel(one, two, out_ref, number_ref, held, row, sems):
    k = held.shape[0]
    number = one[k : k + 1, 0:k] + two[k : k + 1, 0:k]
    row[...] = number
    copies = [pltpu.make_async_copy(row, number_ref, sems.at[OUT_CHUNKS])]
    copies[0].start()
    factor = 1.0 / (column(number) + PRIOR)
    size = k // OUT_CHUNKS
    for i in range(OUT_CHUNKS):
        span = pl.ds(i * size, size)
        held[span, :] = (one[span, :] + two[span, :]) * factor[i * size : (i + 1) * size]
        copies.append(pltpu.make_async_copy(held.at[span], out_ref.at[0, span], sems.at[i]))
        copies[-1].start()
    for copy in copies:
        copy.wait()


def call(kernel, ins, outs, out_specs=VMEM, scratch=(), flops=0, limit=28 << 20, aliases=None):
    return pl.pallas_call(
        kernel,
        out_shape=outs,
        in_specs=ins,
        out_specs=out_specs,
        scratch_shapes=list(scratch),
        input_output_aliases=aliases or {},
        compiler_params=pltpu.CompilerParams(vmem_limit_bytes=limit),
        cost_estimate=pl.CostEstimate(flops=flops, bytes_accessed=1 << 20, transcendentals=0),
    )


class Plan:
    def __init__(self, bit):
        self.mask = 1 << bit
        self.groups = lax.axis_size("group")
        self.subs = lax.axis_size("sub")
        self.chips = self.subs // CORES
        self.bit = bit

    def devices(self):
        for group in range(self.groups):
            for sub in range(self.subs):
                yield group, sub // CORES, sub % CORES, (group >> self.bit) & 1

    def flat(self, group, chip, core):
        return group * self.subs + chip * CORES + core

    def permute(self, value, target):
        pairs = [(self.flat(*device[:3]), self.flat(*target(*device))) for device in self.devices()]
        return lax.ppermute(value, AXES, pairs)

    def seeds(self, value):
        received = []
        for step in range(1, self.chips):
            received.append(
                self.permute(
                    value,
                    lambda group, chip, core, side: (
                        (group, chip ^ step, core)
                        if core == side
                        else (group ^ self.mask, chip ^ (step - 1), 1 - core)
                    ),
                )
            )
        if self.bit >= FAR and self.chips == 2:
            received.append(self.permute(received[0], lambda group, chip, core, side: (group, 1 - chip, core)))
            return received
        received.append(
            self.permute(
                value,
                lambda group, chip, core, side: (
                    (group ^ self.mask, chip ^ (self.chips - 1), core) if core == side else (group, chip, 1 - core)
                ),
            )
        )
        return received

    def sums(self, value):
        moves = [(0, 1 << i) for i in range(self.chips.bit_length() - 1)]
        orders = [moves + [(self.mask, 0)], [(self.mask, 0)] + moves]
        for i in range(len(moves) + 1):
            if i:
                value = merge(*pair)

            def target(group, chip, core, side):
                flip, step = orders[core][i]
                return group ^ flip, chip ^ step, core

            pair = value, self.permute(value, target)
        return pair

    def last_sums(self, value):
        received = [value]
        if self.chips == 2:
            for hub in (0, 1):

                def target(group, chip, core, side):
                    if core != side:
                        return group ^ self.mask, hub, core if chip == 0 else 1 - core
                    return group, 1 - hub, core if chip == hub else 1 - core

                received.append(self.permute(value, target))
            return received
        for step in range(1, self.chips):
            received.append(self.permute(value, lambda group, chip, core, side: (group, chip ^ step, core)))
        for step in range(self.chips):
            received.append(
                self.permute(
                    value,
                    lambda group, chip, core, side: (
                        (group, chip, 1 - core) if core == side else (group ^ self.mask, chip ^ step, core)
                    ),
                )
            )
        return received


def merge(own, other):
    return call(merge_kernel, [VMEM] * 2, jax.ShapeDtypeStruct(own.shape, own.dtype))(own, other)


def swap_cores(value):
    return lax.ppermute(value, "sub", [(sub, sub ^ 1) for sub in range(lax.axis_size("sub"))])


def refine(own_marks, other_marks, own_rows, bit, block):
    plan = Plan(bit)
    other_rows = swap_cores(own_rows)
    rows = own_rows.shape[0]
    k, width = own_marks.shape[0] - TAIL, own_marks.shape[1]
    scale = width / 8.0
    scratch = [
        pltpu.VMEM((CORES, k, width), F32), pltpu.VMEM((CORES, TAIL, k), F32)
    ]
    flops = 8 * rows * k * width

    both = [
        jax.ShapeDtypeStruct((CORES, rows, width), BF16),
        jax.ShapeDtypeStruct((CORES, width, rows), BF16),
        jax.ShapeDtypeStruct((CORES, TAIL, rows), F32),
    ]
    held = call(partial(hold_kernel, 0, block), [VMEM] * 2, both, [VMEM] * 3)(own_rows, own_marks)
    held = call(
        partial(hold_kernel, 1, block), [VMEM] * 5, both, [VMEM] * 3, aliases={2: 0, 3: 1, 4: 2}
    )(other_rows, other_marks, *held)
    payload = jax.ShapeDtypeStruct((k + TAIL, width), BF16)

    def iteration(kernel, inputs, kept):
        return call(
            kernel, [VMEM] * (len(inputs) + len(held)), (payload, jax.ShapeDtypeStruct((k, width), kept)), (VMEM, VMEM),
            scratch, flops,
        )(*inputs, *held)

    seeds = plan.seeds((own_marks + other_marks)[0:k])
    sums, centroids = iteration(
        partial(first_kernel, bit, scale, len(seeds)), [own_marks, other_marks, *seeds], BF16
    )
    for _ in range(ITERS - 1):
        sums, centroids = iteration(
            partial(next_kernel, scale), [centroids, *plan.sums(sums)], F32
        )
    parts = plan.last_sums(sums)
    share = call(
        partial(share_kernel, bit), [VMEM] * (1 + len(parts)), jax.ShapeDtypeStruct((k + TAIL, width), F32)
    )(centroids, *parts)
    return call(
        output_kernel, [VMEM] * 2,
        (jax.ShapeDtypeStruct((1, k, width), F32), jax.ShapeDtypeStruct((1, k), F32)), (HBM, HBM),
        [pltpu.VMEM((k, width), F32), pltpu.VMEM((1, k), F32), pltpu.SemaphoreType.DMA((OUT_CHUNKS + 1,))],
    )(share, swap_cores(share))


def local(embeddings, labels, group_bit, init_index):
    k, width = init_index.shape[1], embeddings.shape[1]
    rows = embeddings.shape[0]
    levels = lax.axis_size("group").bit_length() - 1
    own_marks, own_rows = call(
        seed_kernel, [HBM] * 3,
        (jax.ShapeDtypeStruct((k + TAIL, width), BF16), jax.ShapeDtypeStruct((rows, width), BF16)), (VMEM, VMEM),
        [
            pltpu.VMEM((1, k), jnp.int32),
            pltpu.VMEM((1, labels.shape[0]), jnp.int32),
            pltpu.VMEM((k, width), F32),
            pltpu.SemaphoreType.DMA((CHUNKS + 2,)),
        ], 2 * k * rows * width, SEED_VMEM,
    )(init_index, labels[None], embeddings)
    other_marks = swap_cores(own_marks)
    block = rows // labels.shape[0]
    return lax.switch(
        group_bit[0],
        [partial(refine, bit=bit, block=block) for bit in range(levels)],
        own_marks, other_marks, own_rows,
    )


def solution(mesh):
    return jax.shard_map(
        local,
        mesh=mesh,
        in_specs=(P(("group", "sub"), None), P(("group", "sub")), P(), P("group", None)),
        out_specs=(P("group", None, None), P("group", None)),
        check_vma=False,
    )
```
